512 devices in a mesh: dom: 128 (over z, y, x_hi), off: 4 (over x_lo, core).
Axes of the slice: x: 4 (x_hi: 2, x_lo: 2; x = x_hi * 2 + x_lo), y: 8, z: 8, core: 2. Of those that a mesh axis runs over, the one named last changes fastest.
Arguments:
- contrib: float32 [3072, 2432], P('dom'), may hold values from -6 to 6
- slot_octant: int32 [3072], P('dom'), may hold values from 0 to 2047, as said below
- vlist_src: int32 [2048, 80], P('dom'), may hold values from 0 to 2047, as said below
- vlist_class: int32 [2048, 80], P('dom'), may hold values from 0 to 159, as said below
- translation: float32 [160, 152, 152], P('off'), may hold values from -0.0546875 to 0.0546875
Outputs:
- potential: float32 [2048, 2432], P(('dom', 'off'))
The draws below stay inside these ranges and needn't reach their ends.
Inputs may be any that keep to these rules, and one draw needn't show every extreme that they name: `slot_octant`: slot k < 16 of partition p names octant p * 16 + k; its other slots name octants p * 16 + j with -4 <= j < 20, taken modulo 2048, and each partition has one slot at j = -4 and one at j = 19. vlist_src[t, l] = t + d modulo 2048, where the nonzero offset d, with |d| <= 12, depends only on the class vlist_class[t, l]; some class has d = 12 and some d = -12. `vlist_class`: the 80 classes of one octant are all different, and every class is used by some octant.
All inputs are finite; a program needn't handle non-finite values.
Results may differ from the reference program's by a relative error of at most 0.00007.
Values sent between devices are 32-bit elements; how exact they have to be, the bound alone decides.
A program may use at most 64 MiB of HBM per device.

```python
import jax
import jax.numpy as jnp
from jax import lax

E = 152
R = 16
TGT = 16
SPILL = 4
SLOTS = 24
NOCT = 2048
CLS = 160
VL = 80
N_DOM = 128


def draw_slot_octant(key, part):
    row_ids = jnp.arange(N_DOM * SLOTS, dtype=jnp.int32)
    owner = row_ids // SLOTS
    within = row_ids % SLOTS
    spread = jax.random.randint(key, (N_DOM * SLOTS,), -SPILL, TGT + SPILL, dtype=jnp.int32)
    placed = jnp.where(within < TGT, within, spread)
    placed = jnp.where(within == TGT, -SPILL, placed)
    placed = jnp.where(within == TGT + 1, TGT + SPILL - 1, placed)
    return ((owner * TGT + placed + NOCT) % NOCT).astype(jnp.int32)


def vlist_tables(key):
    base = jax.random.fold_in(key, 4099)
    reach = TGT - SPILL
    steps_all = jnp.arange(2 * reach, dtype=jnp.int32)
    signed = (reach - steps_all // 2) * (1 - 2 * (steps_all % 2))
    shuffled = jax.random.permutation(jax.random.fold_in(base, 1), CLS).astype(jnp.int32)
    class_offset = signed[shuffled % (2 * reach)]
    scores = jax.random.randint(jax.random.fold_in(base, 2), (NOCT, CLS), 0, 2 ** 20, dtype=jnp.int32)
    columns = jnp.arange(CLS, dtype=jnp.int32)
    scores = scores * CLS + columns[None, :]
    forced = shuffled[jnp.arange(NOCT, dtype=jnp.int32) % CLS]
    scores = jnp.where(columns[None, :] == forced[:, None], -1, scores)
    classes = jnp.argsort(scores, axis=1)[:, :VL].astype(jnp.int32)
    rows = jnp.arange(NOCT, dtype=jnp.int32)[:, None]
    sources = ((rows + class_offset[classes] + NOCT) % NOCT).astype(jnp.int32)
    return (classes, sources)


def draw_vlist_class(key, part):
    return vlist_tables(key)[0]


def draw_vlist_src(key, part):
    return vlist_tables(key)[1]


def levels(own_key, dims, cuts, low, high):
    def one(axis_at, blocks):
        draws = jax.random.uniform(jax.random.fold_in(jax.random.fold_in(own_key, 6), axis_at), (blocks,), jnp.float32, low / len(cuts), high / len(cuts))
        return jnp.repeat(jnp.exp(draws), dims[axis_at] // blocks).reshape((-1,) + (1,) * (len(dims) - axis_at - 1))

    gain = one(*cuts[0])
    for cut in cuts[1:]:
        gain = gain * one(*cut)
    return gain


def noise(key, extent, width, bound, shards=(), held_as=jnp.bfloat16):
    gain = levels(key, extent, shards, -0.22, 0.18) if shards else 1.0
    entries = jax.random.normal(key, extent, jnp.float32) * width * gain
    return jnp.minimum(jnp.maximum(entries, -bound), bound).astype(held_as)


def setup_inputs(seed: int = 0) -> dict:
    arg_keys = jax.random.split(jax.random.key(seed), 6)
    return {
        "contrib": noise(arg_keys[0], (N_DOM * SLOTS, E * R), 1.0, 6.0, ((0, 128),), jnp.float32),
        "slot_octant": draw_slot_octant(jax.random.fold_in(arg_keys[5], 71), 0),
        "vlist_src": draw_vlist_src(jax.random.fold_in(arg_keys[5], 71), 0),
        "vlist_class": draw_vlist_class(jax.random.fold_in(arg_keys[5], 71), 0),
        "translation": noise(arg_keys[4], (CLS, E, E), (E * VL) ** -0.5, 0.0546875, ((0, 4),), jnp.float32),
    }


def reference(contrib, slot_octant, vlist_src, vlist_class, translation):
    densities = jax.ops.segment_sum(contrib, slot_octant, num_segments=NOCT)

    def one_target(row_data):
        sources, classes = row_data
        blocks = translation[classes]
        gathered = densities[sources].reshape(VL, E, R)
        result = jnp.einsum("lij,ljr->ir", blocks, gathered, precision=lax.Precision.HIGHEST)
        return result.reshape(E * R)

    return lax.map(one_target, (vlist_src, vlist_class))
```

```python
import jax
import jax.numpy as jnp
from jax import lax
from jax.experimental import pallas as pl
from jax.experimental.pallas import tpu as pltpu
from jax.sharding import PartitionSpec as P

MESH = pl.DeviceIdType.MESH
E = 152
R = 16
TGT = 16
SPILL = 4
REACH = TGT - SPILL
SLOTS = 24
LANES = 128
EP = 160
HALF = EP // 2
TILES = 20
OFFS = 4
GROUP = 8


def block_transpose(v):
    row = lax.broadcasted_iota(jnp.int32, (8, LANES), 0)
    blk = lax.broadcasted_iota(jnp.int32, (8, LANES), 1) // R
    v = jnp.where(
        ((row ^ blk) & 4) == 0, v, pltpu.roll(pltpu.roll(v, 4, 0), LANES // 2, 1)
    )
    for b in (2, 1):
        above = pltpu.roll(pltpu.roll(v, b, 0), LANES - R * b, 1)
        below = pltpu.roll(pltpu.roll(v, 8 - b, 0), R * b, 1)
        moved = jnp.where((row & b) != 0, above, below)
        v = jnp.where(((row ^ blk) & b) == 0, v, moved)
    return v


def split(x):
    hi = x.astype(jnp.bfloat16)
    lo = (x - hi.astype(jnp.float32)).astype(jnp.bfloat16)
    return hi, lo


def kernel(
    parts,
    contrib_ref, slot_ref, src_ref, cls_ref, trans_ref, out_ref,
    cbuf, slots, srcv, clsv, traw, tpack,
    own, halo, yhi, ylo, offs, masks, codes, codes_s,
    sendbuf, recvbuf,
    load_sem, trans_sem, halo_send, halo_recv, fwd_send, fwd_recv, code_sem, rs_send, rs_recv,
):
    dom = lax.axis_index("dom")
    off = lax.axis_index("off")
    core = lax.rem(off, 2)
    octants = TGT * parts
    classes = trans_ref.shape[0]
    groups = classes // GROUP
    left = (lax.rem(dom + parts - 1, parts), lax.rem(off + 2, OFFS))
    right = (lax.rem(dom + 1, parts), lax.rem(off + 2, OFFS))
    mate = (dom, off + 1 - 2 * core)

    barrier = pltpu.get_barrier_semaphore()
    peers = [left, right] + [(dom, lax.rem(off + n, OFFS)) for n in (1, 2, 3)]
    for peer in peers:
        pl.semaphore_signal(barrier, inc=1, device_id=peer, device_id_type=MESH)

    loads = [
        pltpu.make_async_copy(contrib_ref, cbuf.at[:, pl.ds(0, E * R)], load_sem.at[0]),
        pltpu.make_async_copy(slot_ref, slots, load_sem.at[1]),
        pltpu.make_async_copy(src_ref, srcv, load_sem.at[2]),
        pltpu.make_async_copy(cls_ref, clsv, load_sem.at[3]),
    ]
    for copy in loads:
        copy.start()

    def trans_copy(g):
        rows = pl.ds(g * GROUP, GROUP)
        return pltpu.make_async_copy(trans_ref.at[rows], traw.at[rows], trans_sem.at[g])

    for g in range(groups):
        trans_copy(g).start()

    cbuf[:, pl.ds(E * R, LANES)] = jnp.zeros((SLOTS, LANES), jnp.float32)
    row = lax.broadcasted_iota(jnp.int32, (8, LANES), 0)
    loads[0].wait()
    loads[1].wait()
    ids = [
        lax.rem(slots[TGT + s] - (dom * TGT - SPILL) + octants, octants)
        for s in range(SLOTS - TGT)
    ]

    @pl.loop(0, TILES // 2)
    def _(pair):
        for half in range(2):
            g = pair * 2 + half
            lanes = pl.ds(pl.multiple_of(g * LANES, LANES), LANES)
            first = pltpu.roll(cbuf[pl.ds(0, 8), lanes], 4, 0)
            second = pltpu.roll(cbuf[pl.ds(8, 8), lanes], 4, 0)
            table = [
                jnp.where(row >= 4, first, 0.0),
                jnp.where(row < 4, first, second),
                jnp.where(row < 4, second, 0.0),
            ]
            for s in range(SLOTS - TGT):
                spill = jnp.broadcast_to(cbuf[pl.ds(TGT + s, 1), lanes], (8, LANES))
                for b in range(3):
                    table[b] = table[b] + jnp.where(row + 8 * b == ids[s], spill, 0.0)
            for b in range(3):
                own[pl.ds(pl.multiple_of(g * 8, 8), 8), pl.ds(b * LANES, LANES)] = (
                    block_transpose(table[b])
                )

    pl.semaphore_wait(barrier, len(peers))

    half_rows = pl.ds(pl.multiple_of(core * HALF, HALF), HALF)
    sends = []
    for n, (peer, lane) in enumerate(((right, LANES), (left, 0))):
        copy = pltpu.make_async_remote_copy(
            src_ref=own.at[half_rows, pl.ds(lane, 2 * LANES)],
            dst_ref=halo.at[n, half_rows],
            send_sem=halo_send.at[n],
            recv_sem=halo_recv.at[n],
            device_id=peer,
            device_id_type=MESH,
        )
        copy.start()
        sends.append(copy)

    loads[2].wait()
    loads[3].wait()
    target = lax.broadcasted_iota(jnp.int32, srcv.shape, 0) + dom * TGT
    code = lax.rem(srcv[...] - target + (REACH + octants), octants) + 1
    spread = (
        lax.broadcasted_iota(jnp.int32, (TGT, TGT * R), 0)
        == lax.broadcasted_iota(jnp.int32, (TGT, TGT * R), 1) // R
    ).astype(jnp.float32)
    dims = (((0,), (0,)), ((), ()))
    code_l = lax.dot_general(
        code.astype(jnp.float32), spread, dims, preferred_element_type=jnp.float32
    )
    class_l = lax.dot_general(
        (clsv[...] - off * classes).astype(jnp.float32), spread, dims,
        preferred_element_type=jnp.float32,
    )

    @pl.loop(0, classes)
    def _(c):
        found = jnp.max(
            jnp.where(class_l == c.astype(jnp.float32), code_l, 0.0), axis=0, keepdims=True
        )
        offs[pl.ds(c, 1), :] = found
        present = jnp.broadcast_to((found > 0.0).astype(jnp.float32), (16, TGT * R))
        masks[c] = present.astype(jnp.bfloat16)

    start = jnp.max(offs[...], axis=1, keepdims=True).astype(jnp.int32) - 1
    codes[...] = jnp.broadcast_to(jnp.clip(start, 0, 2 * REACH), codes.shape)
    code_copy = pltpu.make_async_copy(codes, codes_s, code_sem)
    code_copy.start()

    @pl.loop(0, groups)
    def _(g):
        trans_copy(g).wait()
        for m in range(GROUP):
            hi, lo = split(traw[g * GROUP + m])
            tpack[g * GROUP + m, pl.ds(0, E), :] = hi
            tpack[g * GROUP + m, pl.ds(EP, E), :] = lo

    code_copy.wait()

    forwards = []
    for n in range(2):
        sends[n].wait_recv()
        copy = pltpu.make_async_remote_copy(
            src_ref=halo.at[n, half_rows],
            dst_ref=halo.at[n, half_rows],
            send_sem=fwd_send.at[n],
            recv_sem=fwd_recv.at[n],
            device_id=mate,
            device_id_type=MESH,
        )
        copy.start()
        forwards.append(copy)
    for copy in forwards:
        copy.wait_recv()

    lane16 = lax.broadcasted_iota(jnp.int32, (16, LANES), 1)

    @pl.loop(0, EP // 16)
    def _(b):
        rows = pl.ds(pl.multiple_of(b * 16, 16), 16)

        def tile(ref, q):
            return ref[rows, pl.ds(q * LANES, LANES)]

        lhalo, rhalo = halo.at[0], halo.at[1]
        window = [
            tile(lhalo, 0),
            tile(lhalo, 1) + tile(own, 0),
            tile(own, 1),
            tile(own, 2) + tile(rhalo, 0),
            tile(rhalo, 1),
        ]
        for s in range(8):
            shift = LANES - R * s
            if s == 0:
                tiles = window
            else:
                rolled = [pltpu.roll(w, shift, 1) for w in window]
                tiles = [jnp.where(lane16 < shift, rolled[q], rolled[q + 1]) for q in range(4)]
            for q, value in enumerate(tiles):
                hi, lo = split(value)
                yhi[s * 5 + q, rows, :] = hi
                ylo[s * 5 + q, rows, :] = lo

    def step(c, acc):
        begin = codes_s[c, 0]
        at = lax.rem(begin, 8) * 5 + begin // 8
        mask = masks[c]

        def sources(ref):
            pieces = [
                (ref[at + n].reshape(EP // 16, 16, LANES) * mask[None, :, n * LANES : (n + 1) * LANES])
                .reshape(EP, LANES)
                for n in range(2)
            ]
            return jnp.concatenate(pieces, axis=1)[:E]

        both = jnp.dot(tpack[c], sources(yhi), preferred_element_type=jnp.float32)
        low = jnp.dot(tpack[c, pl.ds(0, EP), :], sources(ylo), preferred_element_type=jnp.float32)
        return acc + (both[:EP] + (both[EP:] + low))

    acc = lax.fori_loop(0, classes, step, jnp.zeros((EP, TGT * R), jnp.float32))

    lane8 = lax.broadcasted_iota(jnp.int32, (8, LANES), 1)
    for g in range(TILES // 2):
        for h in range(2):
            a, b = (
                acc[(2 * g + n) * 8 : (2 * g + n + 1) * 8, h * LANES : (h + 1) * LANES]
                for n in range(2)
            )
            rows = pl.ds(g * 8, 8)
            sendbuf[2 * h, rows, :] = jnp.where(lane8 < 64, a, pltpu.roll(b, 64, 1))
            sendbuf[2 * h + 1, rows, :] = jnp.where(lane8 < 64, pltpu.roll(a, 64, 1), b)
    finals = []
    for n in (2, 3, 1):
        peer = lax.rem(off + n, OFFS)
        copy = pltpu.make_async_remote_copy(
            src_ref=sendbuf.at[peer],
            dst_ref=recvbuf.at[n],
            send_sem=rs_send.at[n - 1],
            recv_sem=rs_recv.at[n - 1],
            device_id=(dom, peer),
            device_id_type=MESH,
        )
        copy.start()
        finals.append(copy)
    for copy in finals:
        copy.wait_recv()
    for g in range(TILES // 2):
        rows = pl.ds(g * 8, 8)
        total = sendbuf[off, rows, :]
        for n in (1, 2, 3):
            total = total + recvbuf[n, rows, :]
        out_ref[:, pl.ds(2 * g * LANES, LANES)] = block_transpose(total)[: TGT // OFFS]
        if 2 * g + 1 < E // 8:
            other = block_transpose(pltpu.roll(total, 64, 1))
            out_ref[:, pl.ds((2 * g + 1) * LANES, LANES)] = other[: TGT // OFFS]
    for copy in sends + forwards + finals:
        copy.wait_send()


def solution(mesh):
    parts = mesh.shape["dom"]

    def local(contrib, slot_octant, vlist_src, vlist_class, translation):
        classes = translation.shape[0]
        wide = TGT * R
        any_spec = pl.BlockSpec(memory_space=pl.ANY)

        def body(*refs):
            kernel(parts, *refs)

        return pl.pallas_call(
            body,
            out_shape=jax.ShapeDtypeStruct((TGT // OFFS, E * R), jnp.float32),
            in_specs=[any_spec] * 5,
            out_specs=pl.BlockSpec(memory_space=pltpu.VMEM),
            scratch_shapes=[
                pltpu.VMEM((SLOTS, TILES * LANES), jnp.float32),
                pltpu.SMEM((SLOTS,), jnp.int32),
                pltpu.VMEM(vlist_src.shape, jnp.int32),
                pltpu.VMEM(vlist_class.shape, jnp.int32),
                pltpu.VMEM(translation.shape, jnp.float32),
                pltpu.VMEM((classes, 2 * EP, E), jnp.bfloat16),
                pltpu.VMEM((EP, 3 * LANES), jnp.float32),
                pltpu.VMEM((2, EP, 2 * LANES), jnp.float32),
                pltpu.VMEM((40, EP, LANES), jnp.bfloat16),
                pltpu.VMEM((40, EP, LANES), jnp.bfloat16),
                pltpu.VMEM((classes, wide), jnp.float32),
                pltpu.VMEM((classes, 16, wide), jnp.bfloat16),
                pltpu.VMEM((classes, LANES), jnp.int32),
                pltpu.SMEM((classes, LANES), jnp.int32),
                pltpu.VMEM((OFFS, HALF, LANES), jnp.float32),
                pltpu.VMEM((OFFS, HALF, LANES), jnp.float32),
                pltpu.SemaphoreType.DMA((4,)),
                pltpu.SemaphoreType.DMA((classes // GROUP,)),
                pltpu.SemaphoreType.DMA((2,)),
                pltpu.SemaphoreType.DMA((2,)),
                pltpu.SemaphoreType.DMA((2,)),
                pltpu.SemaphoreType.DMA((2,)),
                pltpu.SemaphoreType.DMA(()),
                pltpu.SemaphoreType.DMA((3,)),
                pltpu.SemaphoreType.DMA((3,)),
            ],
            compiler_params=pltpu.CompilerParams(collective_id=0, has_side_effects=True),
        )(contrib, slot_octant, vlist_src, vlist_class, translation)

    return jax.shard_map(
        local,
        mesh=mesh,
        in_specs=(P("dom", None), P("dom"), P("dom", None), P("dom", None), P("off", None, None)),
        out_specs=P(("dom", "off"), None),
        check_vma=False,
    )
```

```python
import jax
import jax.numpy as jnp
from jax import lax
from jax.experimental import pallas as pl
from jax.experimental.pallas import tpu as pltpu
from jax.sharding import PartitionSpec as P

MESH = pl.DeviceIdType.MESH
E = 152
R = 16
TGT = 16
SPILL = 4
REACH = TGT - SPILL
SLOTS = 24
LANES = 128
EP = 160
HALF = EP // 2
TILES = 20
OFFS = 4
GROUP = 8
WIDE = TILES // 2 * LANES
TAIL = EP - LANES


def block_transpose(v):
    row = lax.broadcasted_iota(jnp.int32, (8, LANES), 0)
    blk = lax.broadcasted_iota(jnp.int32, (8, LANES), 1) // R
    v = jnp.where(
        ((row ^ blk) & 4) == 0, v, pltpu.roll(pltpu.roll(v, 4, 0), LANES // 2, 1)
    )
    for b in (2, 1):
        above = pltpu.roll(pltpu.roll(v, b, 0), LANES - R * b, 1)
        below = pltpu.roll(pltpu.roll(v, 8 - b, 0), R * b, 1)
        moved = jnp.where((row & b) != 0, above, below)
        v = jnp.where(((row ^ blk) & b) == 0, v, moved)
    return v


def split(x):
    hi = x.astype(jnp.bfloat16)
    lo = (x - hi.astype(jnp.float32)).astype(jnp.bfloat16)
    return hi, lo


def kernel(
    parts,
    contrib_ref, slot_ref, src_ref, cls_ref, trans_ref, out_ref,
    cbuf, slots, srcv, clsv, traw, tpack,
    own, halo, yhi, ylo, offs, masks, codes, codes_s,
    sendbuf, recvbuf,
    load_sem, trans_sem, halo_send, halo_recv, fwd_send, fwd_recv, code_sem, rs_send, rs_recv,
):
    dom = lax.axis_index("dom")
    off = lax.axis_index("off")
    core = lax.rem(off, 2)
    parity = lax.rem(dom, 2)
    octants = TGT * parts
    classes = trans_ref.shape[0]
    groups = classes // GROUP
    across = lax.rem(off + 2, OFFS)
    mate = (dom, off + 1 - 2 * core)

    barrier = pltpu.get_barrier_semaphore()
    peers = [(lax.rem(dom + n, parts), across) for n in (1, parts - 1)]
    peers += [(dom, lax.rem(off + n, OFFS)) for n in (1, 2, 3)]
    for peer in peers:
        pl.semaphore_signal(barrier, inc=1, device_id=peer, device_id_type=MESH)

    def contrib_copy(start, size, sem):
        lanes = pl.ds(pl.multiple_of(start, LANES), size)
        return pltpu.make_async_copy(contrib_ref.at[:, lanes], cbuf.at[:, lanes], sem)

    loads = [
        contrib_copy(core * (E * R - WIDE), WIDE, load_sem.at[0]),
        pltpu.make_async_copy(slot_ref, slots, load_sem.at[1]),
        contrib_copy((1 - core) * WIDE, E * R - WIDE, load_sem.at[2]),
        pltpu.make_async_copy(src_ref, srcv, load_sem.at[3]),
        pltpu.make_async_copy(cls_ref, clsv, load_sem.at[4]),
    ]
    for copy in loads:
        copy.start()

    def trans_copy(g):
        rows = pl.ds(g * GROUP, GROUP)
        return pltpu.make_async_copy(trans_ref.at[rows], traw.at[rows], trans_sem.at[g])

    cbuf[:, pl.ds(E * R, LANES)] = jnp.zeros((SLOTS, LANES), jnp.float32)
    row = lax.broadcasted_iota(jnp.int32, (8, LANES), 0)
    loads[0].wait()
    loads[1].wait()
    ids = [
        lax.rem(slots[TGT + s] - (dom * TGT - SPILL) + octants, octants)
        for s in range(SLOTS - TGT)
    ]

    def own_half(half):
        for n in range(TILES // 2):
            lanes = pl.ds(pl.multiple_of(half * WIDE, LANES) + n * LANES, LANES)
            points = pl.ds(pl.multiple_of(half * HALF, 8) + n * 8, 8)
            first = pltpu.roll(cbuf[pl.ds(0, 8), lanes], 4, 0)
            second = pltpu.roll(cbuf[pl.ds(8, 8), lanes], 4, 0)
            table = [
                jnp.where(row >= 4, first, 0.0),
                jnp.where(row < 4, first, second),
                jnp.where(row < 4, second, 0.0),
            ]
            for s in range(SLOTS - TGT):
                spill = jnp.broadcast_to(cbuf[pl.ds(TGT + s, 1), lanes], (8, LANES))
                for b in range(3):
                    table[b] = table[b] + jnp.where(row + 8 * b == ids[s], spill, 0.0)
            for b in range(3):
                own[points, pl.ds(b * LANES, LANES)] = block_transpose(table[b])

    own_half(core)
    pl.semaphore_wait(barrier, len(peers))

    half_rows = pl.ds(pl.multiple_of(core * HALF, HALF), HALF)

    def halo_copy(n):
        return pltpu.make_async_remote_copy(
            src_ref=own.at[half_rows, pl.ds(pl.multiple_of((1 - n) * LANES, LANES), 2 * LANES)],
            dst_ref=halo.at[n, half_rows],
            send_sem=halo_send.at[n],
            recv_sem=halo_recv.at[n],
            device_id=(lax.rem(dom + 1 + n * (parts - 2), parts), across),
            device_id_type=MESH,
        )

    sends = [halo_copy(1 - parity), halo_copy(parity)]
    for copy in sends:
        copy.start()
    for g in range(groups):
        trans_copy(g).start()
    loads[2].wait()
    own_half(1 - core)

    loads[3].wait()
    loads[4].wait()
    target = lax.broadcasted_iota(jnp.int32, srcv.shape, 0) + dom * TGT
    code = lax.rem(srcv[...] - target + (REACH + octants), octants) + 1
    spread = (
        lax.broadcasted_iota(jnp.int32, (TGT, TGT * R), 0)
        == lax.broadcasted_iota(jnp.int32, (TGT, TGT * R), 1) // R
    ).astype(jnp.float32)
    dims = (((0,), (0,)), ((), ()))
    code_l = lax.dot_general(
        code.astype(jnp.float32), spread, dims, preferred_element_type=jnp.float32
    )
    class_l = lax.dot_general(
        (clsv[...] - off * classes).astype(jnp.float32), spread, dims,
        preferred_element_type=jnp.float32,
    )

    @pl.loop(0, classes)
    def _(c):
        found = jnp.max(
            jnp.where(class_l == c.astype(jnp.float32), code_l, 0.0), axis=0, keepdims=True
        )
        offs[pl.ds(c, 1), :] = found
        present = jnp.broadcast_to((found > 0.0).astype(jnp.float32), (16, TGT * R))
        masks[c] = present.astype(jnp.bfloat16)

    start = jnp.max(offs[...], axis=1, keepdims=True).astype(jnp.int32) - 1
    codes[...] = jnp.broadcast_to(jnp.clip(start, 0, 2 * REACH), codes.shape)
    code_copy = pltpu.make_async_copy(codes, codes_s, code_sem)
    code_copy.start()

    tpack[...] = jnp.zeros(tpack.shape, jnp.bfloat16)
    pad = jnp.zeros((E, EP - E), jnp.float32)

    @pl.loop(0, groups)
    def _(g):
        trans_copy(g).wait()

        def put(value, lane):
            hi, lo = split(value)
            tpack[g, pl.ds(0, E), pl.ds(lane, LANES)] = hi
            tpack[g, pl.ds(EP, E), pl.ds(lane, LANES)] = lo

        for m in range(GROUP):
            put(traw[g * GROUP + m, :, pl.ds(0, LANES)], m * LANES)
        for m in range(0, GROUP, 4):
            tails = []
            for k in range(4):
                tails += [traw[g * GROUP + m + k, :, pl.ds(LANES, E - LANES)], pad]
            put(jnp.concatenate(tails, axis=1), GROUP * LANES + m * TAIL)

    code_copy.wait()

    def forward_copy(n):
        return pltpu.make_async_remote_copy(
            src_ref=halo.at[n, half_rows],
            dst_ref=halo.at[n, half_rows],
            send_sem=fwd_send.at[n],
            recv_sem=fwd_recv.at[n],
            device_id=mate,
            device_id_type=MESH,
        )

    forwards = [forward_copy(parity), forward_copy(1 - parity)]
    for n in range(2):
        halo_copy(parity if n == 0 else 1 - parity).wait_recv()
        forwards[n].start()
    for copy in forwards:
        copy.wait_recv()

    lane16 = lax.broadcasted_iota(jnp.int32, (16, LANES), 1)
    for b in range(EP // 16):
        rows = pl.ds(b * 16, 16)

        def tile(ref, q):
            return ref[rows, pl.ds(q * LANES, LANES)]

        lhalo, rhalo = halo.at[0], halo.at[1]
        window = [
            tile(lhalo, 0),
            tile(lhalo, 1) + tile(own, 0),
            tile(own, 1),
            tile(own, 2) + tile(rhalo, 0),
            tile(rhalo, 1),
        ]
        for ref, terms in zip((yhi, ylo), zip(*map(split, window))):
            for s in range(8):
                shift = LANES - R * s
                if s == 0:
                    tiles = terms
                else:
                    rolled = [pltpu.roll(w, shift, 1) for w in terms]
                    tiles = [jnp.where(lane16 < shift, rolled[q], rolled[q + 1]) for q in range(4)]
                for q, value in enumerate(tiles):
                    ref[s * 5 + q, rows, :] = value

    def sources(ref, c):
        begin = codes_s[c, 0]
        at = lax.rem(begin, 8) * 5 + begin // 8
        pieces = []
        for n in range(2):
            mask = masks[c, :, pl.ds(n * LANES, LANES)]
            value = ref[at + n].reshape(EP // 16, 16, LANES) * mask[None]
            pieces.append(value.reshape(EP, LANES))
        return jnp.concatenate(pieces, axis=1)

    def stacked(ref, g):
        values = [sources(ref, g * GROUP + m) for m in range(GROUP)]
        return jnp.concatenate([v[:LANES] for v in values] + [v[LANES:] for v in values], axis=0)

    acc = jnp.zeros((EP, TGT * R), jnp.float32)
    for g in range(groups):
        both = jnp.dot(tpack[g], stacked(yhi, g), preferred_element_type=jnp.float32)
        low = jnp.dot(
            tpack[g, pl.ds(0, EP), :], stacked(ylo, g), preferred_element_type=jnp.float32
        )
        acc = acc + (both[:EP] + (both[EP:] + low))

    lane8 = lax.broadcasted_iota(jnp.int32, (8, LANES), 1)
    for g in range(TILES // 2):
        for h in range(2):
            a, b = (
                acc[(2 * g + n) * 8 : (2 * g + n + 1) * 8, h * LANES : (h + 1) * LANES]
                for n in range(2)
            )
            rows = pl.ds(g * 8, 8)
            sendbuf[2 * h, rows, :] = jnp.where(lane8 < 64, a, pltpu.roll(b, 64, 1))
            sendbuf[2 * h + 1, rows, :] = jnp.where(lane8 < 64, pltpu.roll(a, 64, 1), b)
    finals = []
    for n in (2, 3, 1):
        peer = lax.rem(off + n, OFFS)
        copy = pltpu.make_async_remote_copy(
            src_ref=sendbuf.at[peer],
            dst_ref=recvbuf.at[n],
            send_sem=rs_send.at[n - 1],
            recv_sem=rs_recv.at[n - 1],
            device_id=(dom, peer),
            device_id_type=MESH,
        )
        copy.start()
        finals.append(copy)
    for copy in finals:
        copy.wait_recv()
    out_ref[...] = (sendbuf[off] + recvbuf[1]) + (recvbuf[2] + recvbuf[3])
    for copy in sends + forwards + finals:
        copy.wait_send()


def finish(sum_ref, out_ref):
    for g in range(TILES // 2):
        total = sum_ref[pl.ds(g * 8, 8), :]
        for n in range(2):
            if 2 * g + n < E // 8:
                value = block_transpose(total if n == 0 else pltpu.roll(total, 64, 1))
                out_ref[:, pl.ds((2 * g + n) * LANES, LANES)] = value[: TGT // OFFS]


def solution(mesh):
    parts = mesh.shape["dom"]

    def local(contrib, slot_octant, vlist_src, vlist_class, translation):
        classes = translation.shape[0]
        wide = TGT * R
        any_spec = pl.BlockSpec(memory_space=pl.ANY)

        def body(*refs):
            kernel(parts, *refs)

        vmem_spec = pl.BlockSpec(memory_space=pltpu.VMEM)
        total = pl.pallas_call(
            body,
            out_shape=jax.ShapeDtypeStruct((HALF, LANES), jnp.float32),
            in_specs=[any_spec] * 5,
            out_specs=vmem_spec,
            scratch_shapes=[
                pltpu.VMEM((SLOTS, TILES * LANES), jnp.float32),
                pltpu.SMEM((SLOTS,), jnp.int32),
                pltpu.VMEM(vlist_src.shape, jnp.int32),
                pltpu.VMEM(vlist_class.shape, jnp.int32),
                pltpu.VMEM(translation.shape, jnp.float32),
                pltpu.VMEM((classes // GROUP, 2 * EP, GROUP * EP), jnp.bfloat16),
                pltpu.VMEM((EP, 3 * LANES), jnp.float32),
                pltpu.VMEM((2, EP, 2 * LANES), jnp.float32),
                pltpu.VMEM((40, EP, LANES), jnp.bfloat16),
                pltpu.VMEM((40, EP, LANES), jnp.bfloat16),
                pltpu.VMEM((classes, wide), jnp.float32),
                pltpu.VMEM((classes, 16, wide), jnp.bfloat16),
                pltpu.VMEM((classes, LANES), jnp.int32),
                pltpu.SMEM((classes, LANES), jnp.int32),
                pltpu.VMEM((OFFS, HALF, LANES), jnp.float32),
                pltpu.VMEM((OFFS, HALF, LANES), jnp.float32),
                pltpu.SemaphoreType.DMA((5,)),
                pltpu.SemaphoreType.DMA((classes // GROUP,)),
                pltpu.SemaphoreType.DMA((2,)),
                pltpu.SemaphoreType.DMA((2,)),
                pltpu.SemaphoreType.DMA((2,)),
                pltpu.SemaphoreType.DMA((2,)),
                pltpu.SemaphoreType.DMA(()),
                pltpu.SemaphoreType.DMA((3,)),
                pltpu.SemaphoreType.DMA((3,)),
            ],
            compiler_params=pltpu.CompilerParams(collective_id=0, has_side_effects=True),
        )(contrib, slot_octant, vlist_src, vlist_class, translation)
        return pl.pallas_call(
            finish,
            out_shape=jax.ShapeDtypeStruct((TGT // OFFS, E * R), jnp.float32),
            in_specs=[vmem_spec],
            out_specs=vmem_spec,
        )(total)

    return jax.shard_map(
        local,
        mesh=mesh,
        in_specs=(P("dom", None), P("dom"), P("dom", None), P("dom", None), P("off", None, None)),
        out_specs=P(("dom", "off"), None),
        check_vma=False,
    )
```

```python
import jax
import jax.numpy as jnp
from jax import lax
from jax.experimental import pallas as pl
from jax.experimental.pallas import tpu as pltpu
from jax.sharding import PartitionSpec as P

MESH = pl.DeviceIdType.MESH
E = 152
R = 16
TGT = 16
SPILL = 4
REACH = TGT - SPILL
SLOTS = 24
LANES = 128
EP = 160
HALF = EP // 2
TILES = 20
OFFS = 4
GROUP = 8
WIDE = TILES // 2 * LANES
TAIL = EP - LANES


def block_transpose(v):
    row = lax.broadcasted_iota(jnp.int32, (8, LANES), 0)
    blk = lax.broadcasted_iota(jnp.int32, (8, LANES), 1) // R
    v = jnp.where(
        ((row ^ blk) & 4) == 0, v, pltpu.roll(pltpu.roll(v, 4, 0), LANES // 2, 1)
    )
    for b in (2, 1):
        above = pltpu.roll(pltpu.roll(v, b, 0), LANES - R * b, 1)
        below = pltpu.roll(pltpu.roll(v, 8 - b, 0), R * b, 1)
        moved = jnp.where((row & b) != 0, above, below)
        v = jnp.where(((row ^ blk) & b) == 0, v, moved)
    return v


def split(x):
    hi = x.astype(jnp.bfloat16)
    lo = (x - hi.astype(jnp.float32)).astype(jnp.bfloat16)
    return hi, lo


def kernel(
    parts,
    contrib_ref, slot_ref, src_ref, cls_ref, trans_ref, out_ref,
    cbuf, slots, srcv, clsv, traw, tpack,
    own, halo, ywin, offs, masks, codes, codes_s,
    sendbuf, recvbuf,
    load_sem, trans_sem, halo_send, halo_recv, fwd_send, fwd_recv, code_sem, rs_send, rs_recv,
):
    dom = lax.axis_index("dom")
    off = lax.axis_index("off")
    core = lax.rem(off, 2)
    parity = lax.rem(dom, 2)
    octants = TGT * parts
    classes = trans_ref.shape[0]
    groups = classes // GROUP
    across = lax.rem(off + 2, OFFS)
    mate = (dom, off + 1 - 2 * core)

    barrier = pltpu.get_barrier_semaphore()
    peers = [(lax.rem(dom + n, parts), across) for n in (1, parts - 1)]
    peers += [(dom, lax.rem(off + n, OFFS)) for n in (1, 2, 3)]
    for peer in peers:
        pl.semaphore_signal(barrier, inc=1, device_id=peer, device_id_type=MESH)

    def contrib_copy(start, size, sem):
        lanes = pl.ds(pl.multiple_of(start, LANES), size)
        return pltpu.make_async_copy(contrib_ref.at[:, lanes], cbuf.at[:, lanes], sem)

    loads = [
        contrib_copy(core * (E * R - WIDE), WIDE, load_sem.at[0]),
        pltpu.make_async_copy(slot_ref, slots, load_sem.at[1]),
        contrib_copy((1 - core) * WIDE, E * R - WIDE, load_sem.at[2]),
        pltpu.make_async_copy(src_ref, srcv, load_sem.at[3]),
        pltpu.make_async_copy(cls_ref, clsv, load_sem.at[4]),
    ]
    for copy in loads:
        copy.start()

    def trans_copy(g):
        rows = pl.ds(g * GROUP, GROUP)
        return pltpu.make_async_copy(trans_ref.at[rows], traw.at[rows], trans_sem.at[g])

    cbuf[:, pl.ds(E * R, LANES)] = jnp.zeros((SLOTS, LANES), jnp.float32)
    row = lax.broadcasted_iota(jnp.int32, (8, LANES), 0)
    loads[0].wait()
    loads[1].wait()
    ids = [
        lax.rem(slots[TGT + s] - (dom * TGT - SPILL) + octants, octants)
        for s in range(SLOTS - TGT)
    ]

    def own_half(half):
        for n in range(TILES // 2):
            lanes = pl.ds(pl.multiple_of(half * WIDE, LANES) + n * LANES, LANES)
            points = pl.ds(pl.multiple_of(half * HALF, 8) + n * 8, 8)
            first = pltpu.roll(cbuf[pl.ds(0, 8), lanes], 4, 0)
            second = pltpu.roll(cbuf[pl.ds(8, 8), lanes], 4, 0)
            table = [
                jnp.where(row >= 4, first, 0.0),
                jnp.where(row < 4, first, second),
                jnp.where(row < 4, second, 0.0),
            ]
            for s in range(SLOTS - TGT):
                spill = jnp.broadcast_to(cbuf[pl.ds(TGT + s, 1), lanes], (8, LANES))
                for b in range(3):
                    table[b] = table[b] + jnp.where(row + 8 * b == ids[s], spill, 0.0)
            for b in range(3):
                own[points, pl.ds(b * LANES, LANES)] = block_transpose(table[b])

    own_half(core)
    pl.semaphore_wait(barrier, len(peers))

    half_rows = pl.ds(pl.multiple_of(core * HALF, HALF), HALF)

    def halo_copy(n):
        return pltpu.make_async_remote_copy(
            src_ref=own.at[half_rows, pl.ds(pl.multiple_of((1 - n) * LANES, LANES), 2 * LANES)],
            dst_ref=halo.at[n, half_rows],
            send_sem=halo_send.at[n],
            recv_sem=halo_recv.at[n],
            device_id=(lax.rem(dom + 1 + n * (parts - 2), parts), across),
            device_id_type=MESH,
        )

    sends = [halo_copy(1 - parity), halo_copy(parity)]
    for copy in sends:
        copy.start()
    for g in range(groups):
        trans_copy(g).start()
    loads[2].wait()
    own_half(1 - core)

    loads[3].wait()
    loads[4].wait()
    target = lax.broadcasted_iota(jnp.int32, srcv.shape, 0) + dom * TGT
    code = lax.rem(srcv[...] - target + (REACH + octants), octants) + 1
    spread = (
        lax.broadcasted_iota(jnp.int32, (TGT, TGT * R), 0)
        == lax.broadcasted_iota(jnp.int32, (TGT, TGT * R), 1) // R
    ).astype(jnp.float32)
    dims = (((0,), (0,)), ((), ()))
    code_l = lax.dot_general(
        code.astype(jnp.float32), spread, dims, preferred_element_type=jnp.float32
    )
    class_l = lax.dot_general(
        (clsv[...] - off * classes).astype(jnp.float32), spread, dims,
        preferred_element_type=jnp.float32,
    )

    @pl.loop(0, classes)
    def _(c):
        found = jnp.max(
            jnp.where(class_l == c.astype(jnp.float32), code_l, 0.0), axis=0, keepdims=True
        )
        offs[pl.ds(c, 1), :] = found
        present = jnp.broadcast_to((found > 0.0).astype(jnp.float32), (16, TGT * R))
        for n in range(2):
            masks[c, n] = present[:, n * LANES : (n + 1) * LANES].astype(jnp.bfloat16)

    start = jnp.max(offs[...], axis=1, keepdims=True).astype(jnp.int32) - 1
    codes[...] = jnp.broadcast_to(jnp.clip(start, 0, 2 * REACH), codes.shape)
    code_copy = pltpu.make_async_copy(codes, codes_s, code_sem)
    code_copy.start()

    tpack[...] = jnp.zeros(tpack.shape, jnp.bfloat16)
    pad = jnp.zeros((E, EP - E), jnp.float32)

    @pl.loop(0, groups)
    def _(g):
        trans_copy(g).wait()

        def put(value, lane):
            hi, lo = split(value)
            tpack[g, pl.ds(0, E), pl.ds(lane, LANES)] = hi
            tpack[g, pl.ds(EP, E), pl.ds(lane, LANES)] = lo

        for m in range(GROUP):
            put(traw[g * GROUP + m, :, pl.ds(0, LANES)], m * LANES)
        for m in range(0, GROUP, 4):
            tails = []
            for k in range(4):
                tails += [traw[g * GROUP + m + k, :, pl.ds(LANES, E - LANES)], pad]
            put(jnp.concatenate(tails, axis=1), GROUP * LANES + m * TAIL)

    code_copy.wait()

    def forward_copy(n):
        return pltpu.make_async_remote_copy(
            src_ref=halo.at[n, half_rows],
            dst_ref=halo.at[n, half_rows],
            send_sem=fwd_send.at[n],
            recv_sem=fwd_recv.at[n],
            device_id=mate,
            device_id_type=MESH,
        )

    forwards = [forward_copy(parity), forward_copy(1 - parity)]
    for n in range(2):
        halo_copy(parity if n == 0 else 1 - parity).wait_recv()
        forwards[n].start()

    lane16 = lax.broadcasted_iota(jnp.int32, (16, LANES), 1)
    lhalo, rhalo = halo.at[0], halo.at[1]

    def shifted(half):
        for b in range(HALF // 16):
            rows = pl.ds(pl.multiple_of(half * HALF, 16) + b * 16, 16)

            def tile(ref, q):
                return ref[rows, pl.ds(q * LANES, LANES)]

            window = [
                tile(lhalo, 0),
                tile(lhalo, 1) + tile(own, 0),
                tile(own, 1),
                tile(own, 2) + tile(rhalo, 0),
                tile(rhalo, 1),
            ]
            for k, terms in enumerate(zip(*map(split, window))):
                for s in range(8):
                    shift = LANES - R * s
                    if s == 0:
                        tiles = terms
                    else:
                        rolled = [pltpu.roll(w, shift, 1) for w in terms]
                        tiles = [
                            jnp.where(lane16 < shift, rolled[q], rolled[q + 1]) for q in range(4)
                        ]
                    for q, value in enumerate(tiles):
                        ywin[s * 5 + q, rows, pl.ds(k * LANES, LANES)] = value

    shifted(core)
    for copy in forwards:
        copy.wait_recv()
    shifted(1 - core)

    def stacked(g, n):
        values = []
        for c in range(g * GROUP, (g + 1) * GROUP):
            begin = codes_s[c, 0]
            at = lax.rem(begin, 8) * 5 + begin // 8
            mask = masks[c, n]
            both = jnp.concatenate([mask, mask], axis=1)
            value = ywin[at + n].reshape(EP // 16, 16, 2 * LANES) * both[None]
            values.append(value.reshape(EP, 2 * LANES))
        return jnp.concatenate([v[:LANES] for v in values] + [v[LANES:] for v in values], axis=0)

    lane8 = lax.broadcasted_iota(jnp.int32, (8, LANES), 1)

    def partial_sums(n):
        acc = jnp.zeros((EP, LANES), jnp.float32)
        for g in range(groups):
            prod = jnp.dot(tpack[g], stacked(g, n), preferred_element_type=jnp.float32)
            acc = acc + (prod[:EP, :LANES] + (prod[EP:, :LANES] + prod[:EP, LANES:]))
        for g in range(TILES // 2):
            a, b = (acc[(2 * g + k) * 8 : (2 * g + k + 1) * 8] for k in range(2))
            rows = pl.ds(g * 8, 8)
            sendbuf[2 * n, rows, :] = jnp.where(lane8 < 64, a, pltpu.roll(b, 64, 1))
            sendbuf[2 * n + 1, rows, :] = jnp.where(lane8 < 64, pltpu.roll(a, 64, 1), b)

    def final_copy(peer):
        n = lax.rem(peer - off + OFFS, OFFS)
        return pltpu.make_async_remote_copy(
            src_ref=sendbuf.at[peer],
            dst_ref=recvbuf.at[n],
            send_sem=rs_send.at[n - 1],
            recv_sem=rs_recv.at[n - 1],
            device_id=(dom, peer),
            device_id_type=MESH,
        )

    chip = off // 2
    partial_sums(1 - chip)
    finals = [final_copy(2 * (1 - chip) + k) for k in range(2)]
    for copy in finals:
        copy.start()
    partial_sums(chip)
    finals.append(final_copy(2 * chip + 1 - core))
    finals[2].start()
    for n in (1, 2, 3):
        final_copy(lax.rem(off + n, OFFS)).wait_recv()
    out_ref[...] = (sendbuf[off] + recvbuf[1]) + (recvbuf[2] + recvbuf[3])
    for copy in sends + forwards + finals:
        copy.wait_send()


def finish(sum_ref, out_ref):
    for g in range(TILES // 2):
        total = sum_ref[pl.ds(g * 8, 8), :]
        for n in range(2):
            if 2 * g + n < E // 8:
                value = block_transpose(total if n == 0 else pltpu.roll(total, 64, 1))
                out_ref[:, pl.ds((2 * g + n) * LANES, LANES)] = value[: TGT // OFFS]


def solution(mesh):
    parts = mesh.shape["dom"]

    def local(contrib, slot_octant, vlist_src, vlist_class, translation):
        classes = translation.shape[0]
        wide = TGT * R
        hbm_spec = pl.BlockSpec(memory_space=pltpu.HBM)

        args = (contrib, slot_octant, vlist_src, vlist_class, translation)
        args = [pltpu.with_memory_space_constraint(a, pltpu.HBM) for a in args]

        def body(*refs):
            kernel(parts, *refs)

        vmem_spec = pl.BlockSpec(memory_space=pltpu.VMEM)
        total = pl.pallas_call(
            body,
            out_shape=jax.ShapeDtypeStruct((HALF, LANES), jnp.float32),
            in_specs=[hbm_spec] * 5,
            out_specs=vmem_spec,
            scratch_shapes=[
                pltpu.VMEM((SLOTS, TILES * LANES), jnp.float32),
                pltpu.SMEM((SLOTS,), jnp.int32),
                pltpu.VMEM(vlist_src.shape, jnp.int32),
                pltpu.VMEM(vlist_class.shape, jnp.int32),
                pltpu.VMEM(translation.shape, jnp.float32),
                pltpu.VMEM((classes // GROUP, 2 * EP, GROUP * EP), jnp.bfloat16),
                pltpu.VMEM((EP, 3 * LANES), jnp.float32),
                pltpu.VMEM((2, EP, 2 * LANES), jnp.float32),
                pltpu.VMEM((40, EP, 2 * LANES), jnp.bfloat16),
                pltpu.VMEM((classes, wide), jnp.float32),
                pltpu.VMEM((classes, 2, 16, LANES), jnp.bfloat16),
                pltpu.VMEM((classes, LANES), jnp.int32),
                pltpu.SMEM((classes, LANES), jnp.int32),
                pltpu.VMEM((OFFS, HALF, LANES), jnp.float32),
                pltpu.VMEM((OFFS, HALF, LANES), jnp.float32),
                pltpu.SemaphoreType.DMA((5,)),
                pltpu.SemaphoreType.DMA((classes // GROUP,)),
                pltpu.SemaphoreType.DMA((2,)),
                pltpu.SemaphoreType.DMA((2,)),
                pltpu.SemaphoreType.DMA((2,)),
                pltpu.SemaphoreType.DMA((2,)),
                pltpu.SemaphoreType.DMA(()),
                pltpu.SemaphoreType.DMA((3,)),
                pltpu.SemaphoreType.DMA((3,)),
            ],
            compiler_params=pltpu.CompilerParams(
                collective_id=0, has_side_effects=True, vmem_limit_bytes=32 << 20
            ),
        )(*args)
        return pl.pallas_call(
            finish,
            out_shape=jax.ShapeDtypeStruct((TGT // OFFS, E * R), jnp.float32),
            in_specs=[vmem_spec],
            out_specs=vmem_spec,
            compiler_params=pltpu.CompilerParams(vmem_limit_bytes=8 << 20),
        )(total)

    return jax.shard_map(
        local,
        mesh=mesh,
        in_specs=(P("dom", None), P("dom"), P("dom", None), P("dom", None), P("off", None, None)),
        out_specs=P(("dom", "off"), None),
        check_vma=False,
    )
```

```python
import jax
import jax.numpy as jnp
from jax import lax
from jax.experimental import pallas as pl
from jax.experimental.pallas import tpu as pltpu
from jax.sharding import PartitionSpec as P

MESH = pl.DeviceIdType.MESH
E = 152
R = 16
TGT = 16
SPILL = 4
REACH = TGT - SPILL
SLOTS = 24
LANES = 128
EP = 160
HALF = EP // 2
TILES = 20
OFFS = 4
GROUP = 8
WIDE = TILES // 2 * LANES


def block_transpose(v):
    row = lax.broadcasted_iota(jnp.int32, (8, LANES), 0)
    blk = lax.broadcasted_iota(jnp.int32, (8, LANES), 1) // R
    v = jnp.where(
        ((row ^ blk) & 4) == 0, v, pltpu.roll(pltpu.roll(v, 4, 0), LANES // 2, 1)
    )
    for b in (2, 1):
        above = pltpu.roll(pltpu.roll(v, b, 0), LANES - R * b, 1)
        below = pltpu.roll(pltpu.roll(v, 8 - b, 0), R * b, 1)
        moved = jnp.where((row & b) != 0, above, below)
        v = jnp.where(((row ^ blk) & b) == 0, v, moved)
    return v


def split(x):
    hi = x.astype(jnp.bfloat16)
    lo = (x - hi.astype(jnp.float32)).astype(jnp.bfloat16)
    return hi, lo


def kernel(
    parts,
    contrib_ref, slot_ref, src_ref, cls_ref, trans_ref, out_ref,
    cbuf, slots, srcv, clsv, traw, tpack,
    own, halo, ywin, xbuf, offs, masks, codes, codes_s,
    sendbuf, recvbuf,
    load_sem, trans_sem, halo_send, halo_recv, fwd_send, fwd_recv, code_sem, rs_send, rs_recv,
):
    dom = lax.axis_index("dom")
    off = lax.axis_index("off")
    core = lax.rem(off, 2)
    parity = lax.rem(dom, 2)
    octants = TGT * parts
    classes = trans_ref.shape[0]
    groups = classes // GROUP
    across = lax.rem(off + 2, OFFS)
    mate = (dom, off + 1 - 2 * core)

    barrier = pltpu.get_barrier_semaphore()
    peers = [(lax.rem(dom + n, parts), across) for n in (1, parts - 1)]
    peers += [(dom, lax.rem(off + n, OFFS)) for n in (1, 2, 3)]
    for peer in peers:
        pl.semaphore_signal(barrier, inc=1, device_id=peer, device_id_type=MESH)

    def contrib_copy(start, size, sem):
        lanes = pl.ds(pl.multiple_of(start, LANES), size)
        return pltpu.make_async_copy(contrib_ref.at[:, lanes], cbuf.at[:, lanes], sem)

    loads = [
        contrib_copy(core * (E * R - WIDE), WIDE, load_sem.at[0]),
        pltpu.make_async_copy(slot_ref, slots, load_sem.at[1]),
        contrib_copy((1 - core) * WIDE, E * R - WIDE, load_sem.at[2]),
        pltpu.make_async_copy(src_ref, srcv, load_sem.at[3]),
        pltpu.make_async_copy(cls_ref, clsv, load_sem.at[4]),
    ]
    for copy in loads:
        copy.start()

    def trans_copy(g):
        rows = pl.ds(g * GROUP, GROUP)
        return pltpu.make_async_copy(trans_ref.at[rows], traw.at[rows], trans_sem.at[g])

    cbuf[:, pl.ds(E * R, LANES)] = jnp.zeros((SLOTS, LANES), jnp.float32)
    row = lax.broadcasted_iota(jnp.int32, (8, LANES), 0)
    loads[0].wait()
    loads[1].wait()
    ids = [
        lax.rem(slots[TGT + s] - (dom * TGT - SPILL) + octants, octants)
        for s in range(SLOTS - TGT)
    ]

    def own_half(half):
        for n in range(TILES // 2):
            lanes = pl.ds(pl.multiple_of(half * WIDE, LANES) + n * LANES, LANES)
            points = pl.ds(pl.multiple_of(half * HALF, 8) + n * 8, 8)
            first = pltpu.roll(cbuf[pl.ds(0, 8), lanes], 4, 0)
            second = pltpu.roll(cbuf[pl.ds(8, 8), lanes], 4, 0)
            table = [
                jnp.where(row >= 4, first, 0.0),
                jnp.where(row < 4, first, second),
                jnp.where(row < 4, second, 0.0),
            ]
            for s in range(SLOTS - TGT):
                spill = jnp.broadcast_to(cbuf[pl.ds(TGT + s, 1), lanes], (8, LANES))
                for b in range(3):
                    table[b] = table[b] + jnp.where(row + 8 * b == ids[s], spill, 0.0)
            for b in range(3):
                own[points, pl.ds(b * LANES, LANES)] = block_transpose(table[b])

    own_half(core)
    pl.semaphore_wait(barrier, len(peers))

    half_rows = pl.ds(pl.multiple_of(core * HALF, HALF), HALF)

    def halo_copy(n):
        return pltpu.make_async_remote_copy(
            src_ref=own.at[half_rows, pl.ds(pl.multiple_of((1 - n) * LANES, LANES), 2 * LANES)],
            dst_ref=halo.at[n, half_rows],
            send_sem=halo_send.at[n],
            recv_sem=halo_recv.at[n],
            device_id=(lax.rem(dom + 1 + n * (parts - 2), parts), across),
            device_id_type=MESH,
        )

    sends = [halo_copy(1 - parity), halo_copy(parity)]
    for copy in sends:
        copy.start()
    for g in range(groups):
        trans_copy(g).start()
    loads[2].wait()
    own_half(1 - core)

    loads[3].wait()
    loads[4].wait()
    target = lax.broadcasted_iota(jnp.int32, srcv.shape, 0) + dom * TGT
    code = lax.rem(srcv[...] - target + (REACH + octants), octants) + 1
    spread = (
        lax.broadcasted_iota(jnp.int32, (TGT, TGT * R), 0)
        == lax.broadcasted_iota(jnp.int32, (TGT, TGT * R), 1) // R
    ).astype(jnp.float32)
    dims = (((0,), (0,)), ((), ()))
    code_l = lax.dot_general(
        code.astype(jnp.float32), spread, dims, preferred_element_type=jnp.float32
    )
    class_l = lax.dot_general(
        (clsv[...] - off * classes).astype(jnp.float32), spread, dims,
        preferred_element_type=jnp.float32,
    )

    @pl.loop(0, classes)
    def _(c):
        found = jnp.max(
            jnp.where(class_l == c.astype(jnp.float32), code_l, 0.0), axis=0, keepdims=True
        )
        offs[pl.ds(c, 1), :] = found
        present = jnp.broadcast_to((found > 0.0).astype(jnp.float32), (16, TGT * R))
        for n in range(2):
            masks[c, n] = present[:, n * LANES : (n + 1) * LANES].astype(jnp.bfloat16)

    start = jnp.max(offs[...], axis=1, keepdims=True).astype(jnp.int32) - 1
    codes[...] = jnp.broadcast_to(jnp.clip(start, 0, 2 * REACH), codes.shape)
    code_copy = pltpu.make_async_copy(codes, codes_s, code_sem)
    code_copy.start()

    tpack[...] = jnp.zeros(tpack.shape, jnp.bfloat16)
    pad = jnp.zeros((E, EP - E), jnp.float32)

    @pl.loop(0, groups)
    def _(g):
        trans_copy(g).wait()
        lanes = pl.ds(pl.multiple_of(g * (GROUP * HALF), LANES), GROUP * HALF)
        for half in range(2):
            pieces = []
            for m in range(GROUP):
                if half == 0:
                    pieces.append(traw[g * GROUP + m, :, pl.ds(0, HALF)])
                else:
                    pieces += [traw[g * GROUP + m, :, pl.ds(HALF, E - HALF)], pad]
            for k, term in enumerate(split(jnp.concatenate(pieces, axis=1))):
                tpack[half, pl.ds(k * HALF, HALF), lanes] = term[:HALF]
                tpack[half, pl.ds(EP + k * HALF, E - HALF), lanes] = term[HALF:]

    code_copy.wait()

    def forward_copy(n):
        return pltpu.make_async_remote_copy(
            src_ref=halo.at[n, half_rows],
            dst_ref=halo.at[n, half_rows],
            send_sem=fwd_send.at[n],
            recv_sem=fwd_recv.at[n],
            device_id=mate,
            device_id_type=MESH,
        )

    forwards = [forward_copy(parity), forward_copy(1 - parity)]
    for n in range(2):
        halo_copy(parity if n == 0 else 1 - parity).wait_recv()
        forwards[n].start()

    lane16 = lax.broadcasted_iota(jnp.int32, (16, LANES), 1)
    lhalo, rhalo = halo.at[0], halo.at[1]

    def shifted(half):
        for b in range(HALF // 16):
            rows = pl.ds(pl.multiple_of(half * HALF, 16) + b * 16, 16)

            def tile(ref, q):
                return ref[rows, pl.ds(q * LANES, LANES)]

            window = [
                tile(lhalo, 0),
                tile(lhalo, 1) + tile(own, 0),
                tile(own, 1),
                tile(own, 2) + tile(rhalo, 0),
                tile(rhalo, 1),
            ]
            for k, terms in enumerate(zip(*map(split, window))):
                for s in range(8):
                    shift = LANES - R * s
                    if s == 0:
                        tiles = terms
                    else:
                        rolled = [pltpu.roll(w, shift, 1) for w in terms]
                        tiles = [
                            jnp.where(lane16 < shift, rolled[q], rolled[q + 1]) for q in range(4)
                        ]
                    for q, value in enumerate(tiles):
                        ywin[s * 5 + q, rows, pl.ds(k * LANES, LANES)] = value

    def stacked(half, n, chunk):
        values = []
        for c in range(chunk.start, chunk.stop):
            begin = codes_s[c, 0]
            at = lax.rem(begin, 8) * 5 + begin // 8
            mask = masks[c, n]
            both = jnp.concatenate([mask, mask], axis=1)
            rows = pl.ds(pl.multiple_of(half * HALF, 16), HALF)
            value = ywin[at + n, rows, :].reshape(HALF // 16, 16, 2 * LANES) * both[None]
            values.append(value.reshape(HALF, 2 * LANES))
        return jnp.concatenate(values, axis=0)

    def product(half, part, chunk, sources):
        lanes = pl.ds(chunk.start * HALF, len(chunk) * HALF)
        prod = jnp.dot(
            tpack[half, pl.ds(part * EP, EP), lanes], sources, preferred_element_type=jnp.float32
        )
        return prod[:HALF, :LANES] + (prod[HALF:, :LANES] + prod[:HALF, LANES:])

    chunks = [range(c, min(c + 2 * GROUP, classes)) for c in range(0, classes, 2 * GROUP)]

    def whole_product(half, n, sums):
        for chunk in chunks:
            value = stacked(half, n, chunk)
            sums = [sums[part] + product(half, part, chunk, value) for part in range(2)]
        return sums

    lane8 = lax.broadcasted_iota(jnp.int32, (8, LANES), 1)

    def to_send(n, part, value):
        for g in range(HALF // 16):
            a, b = (value[(2 * g + k) * 8 : (2 * g + k + 1) * 8] for k in range(2))
            rows = pl.ds((part * (HALF // 16) + g) * 8, 8)
            sendbuf[2 * n, rows, :] = jnp.where(lane8 < 64, a, pltpu.roll(b, 64, 1))
            sendbuf[2 * n + 1, rows, :] = jnp.where(lane8 < 64, pltpu.roll(a, 64, 1), b)

    def final_copy(peer, part):
        n = lax.rem(peer - off + OFFS, OFFS)
        rows = pl.ds(part * (HALF // 2), HALF // 2)
        return pltpu.make_async_remote_copy(
            src_ref=sendbuf.at[peer, rows],
            dst_ref=recvbuf.at[n, rows],
            send_sem=rs_send.at[n - 1, part],
            recv_sem=rs_recv.at[n - 1, part],
            device_id=(dom, peer),
            device_id_type=MESH,
        )

    chip = off // 2
    zero = jnp.zeros((HALF, LANES), jnp.float32)
    shifted(core)
    sums = whole_product(core, 1 - chip, [zero, zero])
    for copy in forwards:
        copy.wait_recv()
    shifted(1 - core)
    finals = []
    for part in range(2):
        for chunk in chunks:
            rows = pl.ds(chunk.start * HALF, len(chunk) * HALF)
            if part == 0:
                value = stacked(1 - core, 1 - chip, chunk)
                xbuf[rows, :] = value
            else:
                value = xbuf[rows, :]
            sums[part] = sums[part] + product(1 - core, part, chunk, value)
        to_send(1 - chip, part, sums[part])
        for k in range(2):
            finals.append(final_copy(2 * (1 - chip) + k, part))
            finals[-1].start()
    sums = whole_product(core, chip, [zero, zero])
    sums = whole_product(1 - core, chip, sums)
    for part in range(2):
        to_send(chip, part, sums[part])
        finals.append(final_copy(2 * chip + 1 - core, part))
        finals[-1].start()
    for n in (1, 2, 3):
        for part in range(2):
            final_copy(lax.rem(off + n, OFFS), part).wait_recv()
    out_ref[...] = (sendbuf[off] + recvbuf[1]) + (recvbuf[2] + recvbuf[3])
    for copy in sends + forwards + finals:
        copy.wait_send()


def finish(sum_ref, out_ref):
    for g in range(TILES // 2):
        total = sum_ref[pl.ds(g * 8, 8), :]
        for n in range(2):
            if 2 * g + n < E // 8:
                value = block_transpose(total if n == 0 else pltpu.roll(total, 64, 1))
                out_ref[:, pl.ds((2 * g + n) * LANES, LANES)] = value[: TGT // OFFS]


def solution(mesh):
    parts = mesh.shape["dom"]

    def local(contrib, slot_octant, vlist_src, vlist_class, translation):
        classes = translation.shape[0]
        wide = TGT * R
        hbm_spec = pl.BlockSpec(memory_space=pltpu.HBM)

        args = (contrib, slot_octant, vlist_src, vlist_class, translation)
        args = [pltpu.with_memory_space_constraint(a, pltpu.HBM) for a in args]

        def body(*refs):
            kernel(parts, *refs)

        vmem_spec = pl.BlockSpec(memory_space=pltpu.VMEM)
        total = pl.pallas_call(
            body,
            out_shape=jax.ShapeDtypeStruct((HALF, LANES), jnp.float32),
            in_specs=[hbm_spec] * 5,
            out_specs=vmem_spec,
            scratch_shapes=[
                pltpu.VMEM((SLOTS, TILES * LANES), jnp.float32),
                pltpu.SMEM((SLOTS,), jnp.int32),
                pltpu.VMEM(vlist_src.shape, jnp.int32),
                pltpu.VMEM(vlist_class.shape, jnp.int32),
                pltpu.VMEM(translation.shape, jnp.float32),
                pltpu.VMEM((2, 2 * EP, classes * HALF), jnp.bfloat16),
                pltpu.VMEM((EP, 3 * LANES), jnp.float32),
                pltpu.VMEM((2, EP, 2 * LANES), jnp.float32),
                pltpu.VMEM((40, EP, 2 * LANES), jnp.bfloat16),
                pltpu.VMEM((classes * HALF, 2 * LANES), jnp.bfloat16),
                pltpu.VMEM((classes, wide), jnp.float32),
                pltpu.VMEM((classes, 2, 16, LANES), jnp.bfloat16),
                pltpu.VMEM((classes, LANES), jnp.int32),
                pltpu.SMEM((classes, LANES), jnp.int32),
                pltpu.VMEM((OFFS, HALF, LANES), jnp.float32),
                pltpu.VMEM((OFFS, HALF, LANES), jnp.float32),
                pltpu.SemaphoreType.DMA((5,)),
                pltpu.SemaphoreType.DMA((classes // GROUP,)),
                pltpu.SemaphoreType.DMA((2,)),
                pltpu.SemaphoreType.DMA((2,)),
                pltpu.SemaphoreType.DMA((2,)),
                pltpu.SemaphoreType.DMA((2,)),
                pltpu.SemaphoreType.DMA(()),
                pltpu.SemaphoreType.DMA((3, 2)),
                pltpu.SemaphoreType.DMA((3, 2)),
            ],
            compiler_params=pltpu.CompilerParams(
                collective_id=0, has_side_effects=True, vmem_limit_bytes=32 << 20
            ),
        )(*args)
        return pl.pallas_call(
            finish,
            out_shape=jax.ShapeDtypeStruct((TGT // OFFS, E * R), jnp.float32),
            in_specs=[vmem_spec],
            out_specs=vmem_spec,
            compiler_params=pltpu.CompilerParams(vmem_limit_bytes=8 << 20),
        )(total)

    return jax.shard_map(
        local,
        mesh=mesh,
        in_specs=(P("dom", None), P("dom"), P("dom", None), P("dom", None), P("off", None, None)),
        out_specs=P(("dom", "off"), None),
        check_vma=False,
    )
```

```python
import jax
import jax.numpy as jnp
from jax import lax
from jax.experimental import pallas as pl
from jax.experimental.pallas import tpu as pltpu
from jax.sharding import PartitionSpec as P

MESH = pl.DeviceIdType.MESH
E = 152
R = 16
TGT = 16
SPILL = 4
REACH = TGT - SPILL
SLOTS = 24
LANES = 128
EP = 160
HALF = EP // 2
TILES = 20
OFFS = 4
GROUP = 8
CHUNKS = ((0, 48), (48, 32))
WIDE = TILES // 2 * LANES


def block_transpose(v):
    row = lax.broadcasted_iota(jnp.int32, (8, LANES), 0)
    blk = lax.broadcasted_iota(jnp.int32, (8, LANES), 1) // R
    v = jnp.where(
        ((row ^ blk) & 4) == 0, v, pltpu.roll(pltpu.roll(v, 4, 0), LANES // 2, 1)
    )
    for b in (2, 1):
        above = pltpu.roll(pltpu.roll(v, b, 0), LANES - R * b, 1)
        below = pltpu.roll(pltpu.roll(v, 8 - b, 0), R * b, 1)
        moved = jnp.where((row & b) != 0, above, below)
        v = jnp.where(((row ^ blk) & b) == 0, v, moved)
    return v


def split(x):
    hi = x.astype(jnp.bfloat16)
    lo = (x - hi.astype(jnp.float32)).astype(jnp.bfloat16)
    return hi, lo


def kernel(
    parts,
    contrib_ref, slot_ref, src_ref, cls_ref, trans_ref, out_ref,
    cbuf, slots, srcv, clsv, traw, tpack,
    own, halo, ywin, offs, masks, codes, codes_s,
    sendbuf, recvbuf,
    load_sem, trans_sem, halo_send, halo_recv, fwd_send, fwd_recv, code_sem, rs_send, rs_recv,
):
    dom = lax.axis_index("dom")
    off = lax.axis_index("off")
    core = lax.rem(off, 2)
    octants = TGT * parts
    classes = trans_ref.shape[0]
    groups = classes // GROUP
    across = lax.rem(off + 2, OFFS)
    mate = (dom, off + 1 - 2 * core)

    barrier = pltpu.get_barrier_semaphore()
    peers = [(lax.rem(dom + n, parts), across) for n in (1, parts - 1)]
    peers += [(dom, lax.rem(off + n, OFFS)) for n in (1, 2, 3)]
    for peer in peers:
        pl.semaphore_signal(barrier, inc=1, device_id=peer, device_id_type=MESH)

    def contrib_copy(start, size, sem):
        lanes = pl.ds(pl.multiple_of(start, LANES), size)
        return pltpu.make_async_copy(contrib_ref.at[:, lanes], cbuf.at[:, lanes], sem)

    loads = [
        contrib_copy(core * (E * R - WIDE), WIDE, load_sem.at[0]),
        pltpu.make_async_copy(slot_ref, slots, load_sem.at[1]),
        contrib_copy((1 - core) * WIDE, E * R - WIDE, load_sem.at[2]),
        pltpu.make_async_copy(src_ref, srcv, load_sem.at[3]),
        pltpu.make_async_copy(cls_ref, clsv, load_sem.at[4]),
    ]
    for copy in loads:
        copy.start()

    def trans_copy(g):
        rows = pl.ds(g * GROUP, GROUP)
        return pltpu.make_async_copy(trans_ref.at[rows], traw.at[rows], trans_sem.at[g])

    cbuf[:, pl.ds(E * R, LANES)] = jnp.zeros((SLOTS, LANES), jnp.float32)
    row = lax.broadcasted_iota(jnp.int32, (8, LANES), 0)
    loads[0].wait()
    loads[1].wait()
    ids = [
        lax.rem(slots[TGT + s] - (dom * TGT - SPILL) + octants, octants)
        for s in range(SLOTS - TGT)
    ]

    def own_half(half, first_point, points_count):
        for n in range(first_point // 8, (first_point + points_count) // 8):
            lanes = pl.ds(pl.multiple_of(half * WIDE, LANES) + n * LANES, LANES)
            points = pl.ds(pl.multiple_of(half * HALF, 8) + n * 8, 8)
            first = pltpu.roll(cbuf[pl.ds(0, 8), lanes], 4, 0)
            second = pltpu.roll(cbuf[pl.ds(8, 8), lanes], 4, 0)
            table = [
                jnp.where(row >= 4, first, 0.0),
                jnp.where(row < 4, first, second),
                jnp.where(row < 4, second, 0.0),
            ]
            for s in range(SLOTS - TGT):
                spill = jnp.broadcast_to(cbuf[pl.ds(TGT + s, 1), lanes], (8, LANES))
                for b in range(3):
                    table[b] = table[b] + jnp.where(row + 8 * b == ids[s], spill, 0.0)
            for b in range(3):
                own[points, pl.ds(b * LANES, LANES)] = block_transpose(table[b])

    def halo_copy(n, k):
        first_point, count = CHUNKS[k]
        rows = pl.ds(pl.multiple_of(core * HALF, HALF) + first_point, count)
        return pltpu.make_async_remote_copy(
            src_ref=own.at[rows, pl.ds((1 - n) * LANES, 2 * LANES)],
            dst_ref=halo.at[n, rows],
            send_sem=halo_send.at[n, k],
            recv_sem=halo_recv.at[n, k],
            device_id=(lax.rem(dom + (1 if n == 0 else parts - 1), parts), across),
            device_id_type=MESH,
        )

    own_half(core, *CHUNKS[0])
    pl.semaphore_wait(barrier, len(peers))
    sends = [halo_copy(n, k) for n in range(2) for k in range(2)]
    sends[0].start()
    own_half(core, *CHUNKS[1])
    for copy in sends[1:]:
        copy.start()
    for g in range(groups):
        trans_copy(g).start()
    loads[2].wait()
    own_half(1 - core, 0, HALF)

    loads[3].wait()
    loads[4].wait()
    target = lax.broadcasted_iota(jnp.int32, srcv.shape, 0) + dom * TGT
    code = lax.rem(srcv[...] - target + (REACH + octants), octants) + 1
    spread = (
        lax.broadcasted_iota(jnp.int32, (TGT, TGT * R), 0)
        == lax.broadcasted_iota(jnp.int32, (TGT, TGT * R), 1) // R
    ).astype(jnp.float32)
    dims = (((0,), (0,)), ((), ()))
    code_l = lax.dot_general(
        code.astype(jnp.float32), spread, dims, preferred_element_type=jnp.float32
    )
    class_l = lax.dot_general(
        (clsv[...] - off * classes).astype(jnp.float32), spread, dims,
        preferred_element_type=jnp.float32,
    )

    @pl.loop(0, classes)
    def _(c):
        found = jnp.max(
            jnp.where(class_l == c.astype(jnp.float32), code_l, 0.0), axis=0, keepdims=True
        )
        offs[pl.ds(c, 1), :] = found
        present = jnp.broadcast_to((found > 0.0).astype(jnp.float32), (16, TGT * R))
        for n in range(2):
            masks[c, n] = present[:, n * LANES : (n + 1) * LANES].astype(jnp.bfloat16)

    start = jnp.max(offs[...], axis=1, keepdims=True).astype(jnp.int32) - 1
    codes[...] = jnp.broadcast_to(jnp.clip(start, 0, 2 * REACH), codes.shape)
    code_copy = pltpu.make_async_copy(codes, codes_s, code_sem)
    code_copy.start()

    tpack[...] = jnp.zeros(tpack.shape, jnp.bfloat16)

    @pl.loop(0, groups)
    def _(g):
        trans_copy(g).wait()
        for half in range(2):
            for first_point, count in CHUNKS:
                begin = half * HALF + first_point
                size = min(begin + count, E) - begin
                pieces = []
                for m in range(GROUP):
                    pieces.append(traw[g * GROUP + m, :, pl.ds(begin, size)])
                    if size < count:
                        pieces.append(jnp.zeros((E, count - size), jnp.float32))
                lanes = pl.ds(
                    pl.multiple_of(classes * first_point + g * (GROUP * count), LANES),
                    GROUP * count,
                )
                for k, term in enumerate(split(jnp.concatenate(pieces, axis=1))):
                    tpack[half, pl.ds(k * EP, E), lanes] = term

    code_copy.wait()

    def forward_copy(n, k):
        first_point, count = CHUNKS[k]
        rows = pl.ds(pl.multiple_of(core * HALF, HALF) + first_point, count)
        return pltpu.make_async_remote_copy(
            src_ref=halo.at[n, rows],
            dst_ref=halo.at[n, rows],
            send_sem=fwd_send.at[n, k],
            recv_sem=fwd_recv.at[n, k],
            device_id=mate,
            device_id_type=MESH,
        )

    forwards = [[forward_copy(n, k) for n in range(2)] for k in range(2)]

    lane16 = lax.broadcasted_iota(jnp.int32, (16, LANES), 1)
    lhalo, rhalo = halo.at[0], halo.at[1]

    def shifted(half, k):
        first_point, count = CHUNKS[k]
        for b in range(first_point // 16, (first_point + count) // 16):
            rows = pl.ds(pl.multiple_of(half * HALF, 16) + b * 16, 16)

            def tile(ref, q):
                return ref[rows, pl.ds(q * LANES, LANES)]

            window = [
                tile(lhalo, 0),
                tile(lhalo, 1) + tile(own, 0),
                tile(own, 1),
                tile(own, 2) + tile(rhalo, 0),
                tile(rhalo, 1),
            ]
            for term, terms in enumerate(zip(*map(split, window))):
                for s in range(8):
                    shift = LANES - R * s
                    if s == 0:
                        tiles = terms
                    else:
                        rolled = [pltpu.roll(w, shift, 1) for w in terms]
                        tiles = [
                            jnp.where(lane16 < shift, rolled[q], rolled[q + 1]) for q in range(4)
                        ]
                    for q, value in enumerate(tiles):
                        ywin[s * 5 + q, rows, pl.ds(term * LANES, LANES)] = value

    def stacked(half, k, n, chosen):
        first_point, count = CHUNKS[k]
        rows = pl.ds(pl.multiple_of(half * HALF, 16) + first_point, count)
        values = []
        for c in chosen:
            begin = codes_s[c, 0]
            at = lax.rem(begin, 8) * 5 + begin // 8
            mask = masks[c, n]
            both = jnp.concatenate([mask, mask], axis=1)
            value = ywin[at + n, rows, :].reshape(count // 16, 16, 2 * LANES) * both[None]
            values.append(value.reshape(count, 2 * LANES))
        return jnp.concatenate(values, axis=0)

    def product(half, k, n, total):
        first_point, count = CHUNKS[k]
        for c in range(0, classes, 2 * GROUP):
            chosen = range(c, min(c + 2 * GROUP, classes))
            lanes = pl.ds(classes * first_point + c * count, len(chosen) * count)
            prod = jnp.dot(
                tpack[half, :, lanes], stacked(half, k, n, chosen),
                preferred_element_type=jnp.float32,
            )
            total = total + (prod[:EP, :LANES] + (prod[EP:, :LANES] + prod[:EP, LANES:]))
        return total

    lane8 = lax.broadcasted_iota(jnp.int32, (8, LANES), 1)

    def to_send(n, value):
        for g in range(TILES // 2):
            a, b = (value[(2 * g + k) * 8 : (2 * g + k + 1) * 8] for k in range(2))
            rows = pl.ds(g * 8, 8)
            sendbuf[2 * n, rows, :] = jnp.where(lane8 < 64, a, pltpu.roll(b, 64, 1))
            sendbuf[2 * n + 1, rows, :] = jnp.where(lane8 < 64, pltpu.roll(a, 64, 1), b)

    def final_copy(peer):
        n = lax.rem(peer - off + OFFS, OFFS)
        return pltpu.make_async_remote_copy(
            src_ref=sendbuf.at[peer],
            dst_ref=recvbuf.at[n],
            send_sem=rs_send.at[n - 1],
            recv_sem=rs_recv.at[n - 1],
            device_id=(dom, peer),
            device_id_type=MESH,
        )

    chip = off // 2
    total = jnp.zeros((EP, LANES), jnp.float32)
    for k in range(2):
        for n in range(2):
            sends[2 * n + k].wait_recv()
            forwards[k][n].start()
        shifted(core, k)
        total = product(core, k, 1 - chip, total)
    for k in range(2):
        for copy in forwards[k]:
            copy.wait_recv()
        shifted(1 - core, k)
        total = product(1 - core, k, 1 - chip, total)
    to_send(1 - chip, total)
    finals = [final_copy(2 * (1 - chip) + k) for k in range(2)]
    for copy in finals:
        copy.start()
    total = jnp.zeros((EP, LANES), jnp.float32)
    for half in range(2):
        for k in range(2):
            total = product(half, k, chip, total)
    to_send(chip, total)
    finals.append(final_copy(2 * chip + 1 - core))
    finals[2].start()
    for n in (1, 2, 3):
        final_copy(lax.rem(off + n, OFFS)).wait_recv()
    out_ref[...] = (sendbuf[off] + recvbuf[1]) + (recvbuf[2] + recvbuf[3])
    for copy in sends + forwards[0] + forwards[1] + finals:
        copy.wait_send()


def finish(sum_ref, out_ref):
    for g in range(TILES // 2):
        total = sum_ref[pl.ds(g * 8, 8), :]
        for n in range(2):
            if 2 * g + n < E // 8:
                value = block_transpose(total if n == 0 else pltpu.roll(total, 64, 1))
                out_ref[:, pl.ds((2 * g + n) * LANES, LANES)] = value[: TGT // OFFS]


def solution(mesh):
    parts = mesh.shape["dom"]

    def local(contrib, slot_octant, vlist_src, vlist_class, translation):
        classes = translation.shape[0]
        wide = TGT * R
        hbm_spec = pl.BlockSpec(memory_space=pltpu.HBM)

        args = (contrib, slot_octant, vlist_src, vlist_class, translation)
        args = [pltpu.with_memory_space_constraint(a, pltpu.HBM) for a in args]

        def body(*refs):
            kernel(parts, *refs)

        vmem_spec = pl.BlockSpec(memory_space=pltpu.VMEM)
        total = pl.pallas_call(
            body,
            out_shape=jax.ShapeDtypeStruct((HALF, LANES), jnp.float32),
            in_specs=[hbm_spec] * 5,
            out_specs=vmem_spec,
            scratch_shapes=[
                pltpu.VMEM((SLOTS, TILES * LANES), jnp.float32),
                pltpu.SMEM((SLOTS,), jnp.int32),
                pltpu.VMEM(vlist_src.shape, jnp.int32),
                pltpu.VMEM(vlist_class.shape, jnp.int32),
                pltpu.VMEM(translation.shape, jnp.float32),
                pltpu.VMEM((2, 2 * EP, classes * HALF), jnp.bfloat16),
                pltpu.VMEM((EP, 3 * LANES), jnp.float32),
                pltpu.VMEM((2, EP, 2 * LANES), jnp.float32),
                pltpu.VMEM((40, EP, 2 * LANES), jnp.bfloat16),
                pltpu.VMEM((classes, wide), jnp.float32),
                pltpu.VMEM((classes, 2, 16, LANES), jnp.bfloat16),
                pltpu.VMEM((classes, LANES), jnp.int32),
                pltpu.SMEM((classes, LANES), jnp.int32),
                pltpu.VMEM((OFFS, HALF, LANES), jnp.float32),
                pltpu.VMEM((OFFS, HALF, LANES), jnp.float32),
                pltpu.SemaphoreType.DMA((5,)),
                pltpu.SemaphoreType.DMA((classes // GROUP,)),
                pltpu.SemaphoreType.DMA((2, 2)),
                pltpu.SemaphoreType.DMA((2, 2)),
                pltpu.SemaphoreType.DMA((2, 2)),
                pltpu.SemaphoreType.DMA((2, 2)),
                pltpu.SemaphoreType.DMA(()),
                pltpu.SemaphoreType.DMA((3,)),
                pltpu.SemaphoreType.DMA((3,)),
            ],
            compiler_params=pltpu.CompilerParams(
                collective_id=0, has_side_effects=True, vmem_limit_bytes=32 << 20
            ),
        )(*args)
        return pl.pallas_call(
            finish,
            out_shape=jax.ShapeDtypeStruct((TGT // OFFS, E * R), jnp.float32),
            in_specs=[vmem_spec],
            out_specs=vmem_spec,
            compiler_params=pltpu.CompilerParams(vmem_limit_bytes=8 << 20),
        )(total)

    return jax.shard_map(
        local,
        mesh=mesh,
        in_specs=(P("dom", None), P("dom"), P("dom", None), P("dom", None), P("off", None, None)),
        out_specs=P(("dom", "off"), None),
        check_vma=False,
    )
```

```python
import jax
import jax.numpy as jnp
from jax import lax
from jax.experimental import pallas as pl
from jax.experimental.pallas import tpu as pltpu
from jax.sharding import PartitionSpec as P

MESH = pl.DeviceIdType.MESH
E = 152
R = 16
TGT = 16
SPILL = 4
REACH = TGT - SPILL
SLOTS = 24
LANES = 128
EP = 160
HALF = EP // 2
TILES = 20
OFFS = 4
GROUP = 8
CHUNKS = ((0, HALF),)
WIDE = TILES // 2 * LANES


def block_transpose(v):
    row = lax.broadcasted_iota(jnp.int32, (8, LANES), 0)
    blk = lax.broadcasted_iota(jnp.int32, (8, LANES), 1) // R
    v = jnp.where(
        ((row ^ blk) & 4) == 0, v, pltpu.roll(pltpu.roll(v, 4, 0), LANES // 2, 1)
    )
    for b in (2, 1):
        above = pltpu.roll(pltpu.roll(v, b, 0), LANES - R * b, 1)
        below = pltpu.roll(pltpu.roll(v, 8 - b, 0), R * b, 1)
        moved = jnp.where((row & b) != 0, above, below)
        v = jnp.where(((row ^ blk) & b) == 0, v, moved)
    return v


def split(x):
    hi = x.astype(jnp.bfloat16)
    lo = (x - hi.astype(jnp.float32)).astype(jnp.bfloat16)
    return hi, lo


def kernel(
    parts,
    contrib_ref, slot_ref, src_ref, cls_ref, trans_ref, out_ref,
    cbuf, slots, srcv, clsv, traw, tpack,
    own, halo, ywin, offs, masks, codes, codes_s,
    sendbuf, recvbuf,
    load_sem, trans_sem, halo_send, halo_recv, fwd_send, fwd_recv, code_sem, rs_send, rs_recv,
):
    dom = lax.axis_index("dom")
    off = lax.axis_index("off")
    core = lax.rem(off, 2)
    octants = TGT * parts
    classes = trans_ref.shape[0]
    groups = classes // GROUP
    across = lax.rem(off + 2, OFFS)
    mate = (dom, off + 1 - 2 * core)

    barrier = pltpu.get_barrier_semaphore()
    peers = [(lax.rem(dom + n, parts), across) for n in (1, parts - 1)]
    peers += [(dom, lax.rem(off + n, OFFS)) for n in (1, 2, 3)]
    for peer in peers:
        pl.semaphore_signal(barrier, inc=1, device_id=peer, device_id_type=MESH)

    def contrib_copy(start, size, sem):
        lanes = pl.ds(pl.multiple_of(start, LANES), size)
        return pltpu.make_async_copy(contrib_ref.at[:, lanes], cbuf.at[:, lanes], sem)

    loads = [
        contrib_copy(core * (E * R - WIDE), WIDE, load_sem.at[0]),
        pltpu.make_async_copy(slot_ref, slots, load_sem.at[1]),
        contrib_copy((1 - core) * WIDE, E * R - WIDE, load_sem.at[2]),
        pltpu.make_async_copy(src_ref, srcv, load_sem.at[3]),
        pltpu.make_async_copy(cls_ref, clsv, load_sem.at[4]),
    ]
    for copy in loads:
        copy.start()

    def trans_copy(g):
        rows = pl.ds(g * GROUP, GROUP)
        return pltpu.make_async_copy(trans_ref.at[rows], traw.at[rows], trans_sem.at[g])

    for g in range(groups):
        trans_copy(g).start()

    cbuf[:, pl.ds(E * R, LANES)] = jnp.zeros((SLOTS, LANES), jnp.float32)
    row = lax.broadcasted_iota(jnp.int32, (8, LANES), 0)
    loads[0].wait()
    loads[1].wait()
    ids = [
        lax.rem(slots[TGT + s] - (dom * TGT - SPILL) + octants, octants)
        for s in range(SLOTS - TGT)
    ]

    def own_half(half, first_point, points_count):
        for n in range(first_point // 8, (first_point + points_count) // 8):
            lanes = pl.ds(pl.multiple_of(half * WIDE, LANES) + n * LANES, LANES)
            points = pl.ds(pl.multiple_of(half * HALF, 8) + n * 8, 8)
            first = pltpu.roll(cbuf[pl.ds(0, 8), lanes], 4, 0)
            second = pltpu.roll(cbuf[pl.ds(8, 8), lanes], 4, 0)
            table = [
                jnp.where(row >= 4, first, 0.0),
                jnp.where(row < 4, first, second),
                jnp.where(row < 4, second, 0.0),
            ]
            for s in range(SLOTS - TGT):
                spill = jnp.broadcast_to(cbuf[pl.ds(TGT + s, 1), lanes], (8, LANES))
                for b in range(3):
                    table[b] = table[b] + jnp.where(row + 8 * b == ids[s], spill, 0.0)
            for b in range(3):
                own[points, pl.ds(b * LANES, LANES)] = block_transpose(table[b])

    def halo_copy(n, k):
        first_point, count = CHUNKS[k]
        rows = pl.ds(pl.multiple_of(core * HALF, HALF) + first_point, count)
        return pltpu.make_async_remote_copy(
            src_ref=own.at[rows, pl.ds((1 - n) * LANES, 2 * LANES)],
            dst_ref=halo.at[n, rows],
            send_sem=halo_send.at[n, k],
            recv_sem=halo_recv.at[n, k],
            device_id=(lax.rem(dom + (1 if n == 0 else parts - 1), parts), across),
            device_id_type=MESH,
        )

    def prepare():
        loads[2].wait()
        own_half(1 - core, 0, HALF)

        loads[3].wait()
        loads[4].wait()
        target = lax.broadcasted_iota(jnp.int32, srcv.shape, 0) + dom * TGT
        code = lax.rem(srcv[...] - target + (REACH + octants), octants) + 1
        spread = (
            lax.broadcasted_iota(jnp.int32, (TGT, TGT * R), 0)
            == lax.broadcasted_iota(jnp.int32, (TGT, TGT * R), 1) // R
        ).astype(jnp.float32)
        dims = (((0,), (0,)), ((), ()))
        code_l = lax.dot_general(
            code.astype(jnp.float32), spread, dims, preferred_element_type=jnp.float32
        )
        class_l = lax.dot_general(
            (clsv[...] - off * classes).astype(jnp.float32), spread, dims,
            preferred_element_type=jnp.float32,
        )

        @pl.loop(0, classes)
        def _(c):
            found = jnp.max(
                jnp.where(class_l == c.astype(jnp.float32), code_l, 0.0), axis=0, keepdims=True
            )
            offs[pl.ds(c, 1), :] = found
            present = jnp.broadcast_to((found > 0.0).astype(jnp.float32), (16, TGT * R))
            for n in range(2):
                masks[c, n] = present[:, n * LANES : (n + 1) * LANES].astype(jnp.bfloat16)

        start = jnp.max(offs[...], axis=1, keepdims=True).astype(jnp.int32) - 1
        codes[...] = jnp.broadcast_to(jnp.clip(start, 0, 2 * REACH), codes.shape)
        code_copy = pltpu.make_async_copy(codes, codes_s, code_sem)
        code_copy.start()

        tpack[...] = jnp.zeros(tpack.shape, jnp.bfloat16)

        @pl.loop(0, groups)
        def _(g):
            trans_copy(g).wait()
            for half in range(2):
                for first_point, count in CHUNKS:
                    begin = half * HALF + first_point
                    size = min(begin + count, E) - begin
                    pieces = []
                    for m in range(GROUP):
                        pieces.append(traw[g * GROUP + m, :, pl.ds(begin, size)])
                        if size < count:
                            pieces.append(jnp.zeros((E, count - size), jnp.float32))
                    lanes = pl.ds(
                        pl.multiple_of(classes * first_point + g * (GROUP * count), LANES),
                        GROUP * count,
                    )
                    for k, term in enumerate(split(jnp.concatenate(pieces, axis=1))):
                        tpack[half, pl.ds(k * EP, E), lanes] = term

        code_copy.wait()

    own_half(core, 0, HALF)
    pl.when(dom == 0)(prepare)
    pl.semaphore_wait(barrier, len(peers))
    sends = [halo_copy(n, 0) for n in range(2)]
    for copy in sends:
        copy.start()
    pl.when(dom != 0)(prepare)

    def forward_copy(n, k):
        first_point, count = CHUNKS[k]
        rows = pl.ds(pl.multiple_of(core * HALF, HALF) + first_point, count)
        return pltpu.make_async_remote_copy(
            src_ref=halo.at[n, rows],
            dst_ref=halo.at[n, rows],
            send_sem=fwd_send.at[n, k],
            recv_sem=fwd_recv.at[n, k],
            device_id=mate,
            device_id_type=MESH,
        )

    forwards = [[forward_copy(n, k) for n in range(2)] for k in range(len(CHUNKS))]

    lane16 = lax.broadcasted_iota(jnp.int32, (16, LANES), 1)
    lhalo, rhalo = halo.at[0], halo.at[1]

    def shifted(half, k, left):
        first_point, count = CHUNKS[k]
        for b in range(first_point // 16, (first_point + count) // 16):
            rows = pl.ds(pl.multiple_of(half * HALF, 16) + b * 16, 16)

            def tile(ref, q):
                return ref[rows, pl.ds(q * LANES, LANES)]

            if left:
                first_tile = 0
                window = [tile(lhalo, 0), tile(lhalo, 1) + tile(own, 0), tile(own, 1)]
            else:
                first_tile = 2
                window = [tile(own, 1), tile(own, 2) + tile(rhalo, 0), tile(rhalo, 1)]
            for term, terms in enumerate(zip(*map(split, window))):
                for s in range(8):
                    shift = LANES - R * s
                    if s == 0:
                        tiles = terms[:2] if left else terms
                    else:
                        rolled = [pltpu.roll(w, shift, 1) for w in terms]
                        tiles = [
                            jnp.where(lane16 < shift, rolled[q], rolled[q + 1]) for q in range(2)
                        ]
                    for q, value in enumerate(tiles):
                        ywin[s * 5 + first_tile + q, rows, pl.ds(term * LANES, LANES)] = value

    def stacked(half, k, n, chosen):
        first_point, count = CHUNKS[k]
        rows = pl.ds(pl.multiple_of(half * HALF, 16) + first_point, count)
        values = []
        for c in chosen:
            begin = codes_s[c, 0]
            at = lax.rem(begin, 8) * 5 + begin // 8
            mask = masks[c, n]
            both = jnp.concatenate([mask, mask], axis=1)
            value = ywin[at + n, rows, :].reshape(count // 16, 16, 2 * LANES) * both[None]
            values.append(value.reshape(count, 2 * LANES))
        return jnp.concatenate(values, axis=0)

    def product(half, k, n, total):
        first_point, count = CHUNKS[k]
        for c in range(0, classes, 2 * GROUP):
            chosen = range(c, min(c + 2 * GROUP, classes))
            lanes = pl.ds(classes * first_point + c * count, len(chosen) * count)
            prod = jnp.dot(
                tpack[half, :, lanes], stacked(half, k, n, chosen),
                preferred_element_type=jnp.float32,
            )
            total = total + (prod[:EP, :LANES] + (prod[EP:, :LANES] + prod[:EP, LANES:]))
        return total

    lane8 = lax.broadcasted_iota(jnp.int32, (8, LANES), 1)

    def to_send(n, value):
        for g in range(TILES // 2):
            a, b = (value[(2 * g + k) * 8 : (2 * g + k + 1) * 8] for k in range(2))
            rows = pl.ds(g * 8, 8)
            sendbuf[2 * n, rows, :] = jnp.where(lane8 < 64, a, pltpu.roll(b, 64, 1))
            sendbuf[2 * n + 1, rows, :] = jnp.where(lane8 < 64, pltpu.roll(a, 64, 1), b)

    def final_copy(peer):
        n = lax.rem(peer - off + OFFS, OFFS)
        return pltpu.make_async_remote_copy(
            src_ref=sendbuf.at[peer],
            dst_ref=recvbuf.at[n],
            send_sem=rs_send.at[n - 1],
            recv_sem=rs_recv.at[n - 1],
            device_id=(dom, peer),
            device_id_type=MESH,
        )

    chip = off // 2
    total = jnp.zeros((EP, LANES), jnp.float32)
    for n in (1, 0):
        sends[n].wait_recv()
        forwards[0][n].start()
        shifted(core, 0, n == 0)
        if n == 0:
            total = product(core, 0, 1 - chip, total)
        forwards[0][n].wait_recv()
        shifted(1 - core, 0, n == 0)
    total = product(1 - core, 0, 1 - chip, total)
    to_send(1 - chip, total)
    finals = [final_copy(2 * (1 - chip) + k) for k in (1, 0)]
    for copy in finals:
        copy.start()
    total = jnp.zeros((EP, LANES), jnp.float32)
    for half in range(2):
        for k in range(len(CHUNKS)):
            total = product(half, k, chip, total)
    to_send(chip, total)
    finals.append(final_copy(2 * chip + 1 - core))
    finals[2].start()
    for n in (1, 2, 3):
        final_copy(lax.rem(off + n, OFFS)).wait_recv()
    out_ref[...] = (sendbuf[off] + recvbuf[1]) + (recvbuf[2] + recvbuf[3])
    for copy in sends + forwards[0] + finals:
        copy.wait_send()


def finish(sum_ref, out_ref):
    for g in range(TILES // 2):
        value = block_transpose(sum_ref[pl.ds(g * 8, 8), :])
        for n in range(2):
            if 2 * g + n < E // 8:
                rows = value[n * TGT // OFFS : (n + 1) * TGT // OFFS]
                out_ref[:, pl.ds((2 * g + n) * LANES, LANES)] = rows


def solution(mesh):
    parts = mesh.shape["dom"]

    def local(contrib, slot_octant, vlist_src, vlist_class, translation):
        classes = translation.shape[0]
        wide = TGT * R
        hbm_spec = pl.BlockSpec(memory_space=pltpu.HBM)

        args = (contrib, slot_octant, vlist_src, vlist_class, translation)
        args = [pltpu.with_memory_space_constraint(a, pltpu.HBM) for a in args]

        def body(*refs):
            kernel(parts, *refs)

        vmem_spec = pl.BlockSpec(memory_space=pltpu.VMEM)
        total = pl.pallas_call(
            body,
            out_shape=jax.ShapeDtypeStruct((HALF, LANES), jnp.float32),
            in_specs=[hbm_spec] * 5,
            out_specs=vmem_spec,
            scratch_shapes=[
                pltpu.VMEM((SLOTS, TILES * LANES), jnp.float32),
                pltpu.SMEM((SLOTS,), jnp.int32),
                pltpu.VMEM(vlist_src.shape, jnp.int32),
                pltpu.VMEM(vlist_class.shape, jnp.int32),
                pltpu.VMEM(translation.shape, jnp.float32),
                pltpu.VMEM((2, 2 * EP, classes * HALF), jnp.bfloat16),
                pltpu.VMEM((EP, 3 * LANES), jnp.float32),
                pltpu.VMEM((2, EP, 2 * LANES), jnp.float32),
                pltpu.VMEM((40, EP, 2 * LANES), jnp.bfloat16),
                pltpu.VMEM((classes, wide), jnp.float32),
                pltpu.VMEM((classes, 2, 16, LANES), jnp.bfloat16),
                pltpu.VMEM((classes, LANES), jnp.int32),
                pltpu.SMEM((classes, LANES), jnp.int32),
                pltpu.VMEM((OFFS, HALF, LANES), jnp.float32),
                pltpu.VMEM((OFFS, HALF, LANES), jnp.float32),
                pltpu.SemaphoreType.DMA((5,)),
                pltpu.SemaphoreType.DMA((classes // GROUP,)),
                pltpu.SemaphoreType.DMA((2, 2)),
                pltpu.SemaphoreType.DMA((2, 2)),
                pltpu.SemaphoreType.DMA((2, 2)),
                pltpu.SemaphoreType.DMA((2, 2)),
                pltpu.SemaphoreType.DMA(()),
                pltpu.SemaphoreType.DMA((3,)),
                pltpu.SemaphoreType.DMA((3,)),
            ],
            compiler_params=pltpu.CompilerParams(
                collective_id=0, has_side_effects=True, vmem_limit_bytes=32 << 20
            ),
        )(*args)
        return pl.pallas_call(
            finish,
            out_shape=jax.ShapeDtypeStruct((TGT // OFFS, E * R), jnp.float32),
            in_specs=[vmem_spec],
            out_specs=vmem_spec,
            compiler_params=pltpu.CompilerParams(vmem_limit_bytes=8 << 20),
        )(total)

    return jax.shard_map(
        local,
        mesh=mesh,
        in_specs=(P("dom", None), P("dom"), P("dom", None), P("dom", None), P("off", None, None)),
        out_specs=P(("dom", "off"), None),
        check_vma=False,
    )
```

```python
import jax
import jax.numpy as jnp
from jax import lax
from jax.experimental import pallas as pl
from jax.experimental.pallas import tpu as pltpu
from jax.sharding import PartitionSpec as P

MESH = pl.DeviceIdType.MESH
E = 152
R = 16
TGT = 16
SPILL = 4
REACH = TGT - SPILL
SLOTS = 24
LANES = 128
EP = 160
HALF = EP // 2
TILES = 20
OFFS = 4
GROUP = 8
CHUNKS = ((0, HALF),)
WIDE = TILES // 2 * LANES


def block_transpose(v):
    row = lax.broadcasted_iota(jnp.int32, (8, LANES), 0)
    blk = lax.broadcasted_iota(jnp.int32, (8, LANES), 1) // R
    v = jnp.where(
        ((row ^ blk) & 4) == 0, v, pltpu.roll(pltpu.roll(v, 4, 0), LANES // 2, 1)
    )
    for b in (2, 1):
        above = pltpu.roll(pltpu.roll(v, b, 0), LANES - R * b, 1)
        below = pltpu.roll(pltpu.roll(v, 8 - b, 0), R * b, 1)
        moved = jnp.where((row & b) != 0, above, below)
        v = jnp.where(((row ^ blk) & b) == 0, v, moved)
    return v


def split(x):
    hi = x.astype(jnp.bfloat16)
    lo = (x - hi.astype(jnp.float32)).astype(jnp.bfloat16)
    return hi, lo


def kernel(
    parts,
    contrib_ref, slot_ref, src_ref, cls_ref, trans_ref, out_ref,
    cbuf, slots, srcv, clsv, traw, tpack,
    own, halo, ywin, offs, masks, codes, codes_s,
    sendbuf, recvbuf,
    load_sem, trans_sem, halo_send, halo_recv, fwd_send, fwd_recv, code_sem, rs_send, rs_recv,
):
    dom = lax.axis_index("dom")
    off = lax.axis_index("off")
    core = lax.rem(off, 2)
    octants = TGT * parts
    classes = trans_ref.shape[0]
    groups = classes // GROUP
    across = lax.rem(off + 2, OFFS)
    mate = (dom, off + 1 - 2 * core)

    barrier = pltpu.get_barrier_semaphore()
    peers = [(lax.rem(dom + n, parts), across) for n in (1, parts - 1)]
    peers += [(dom, lax.rem(off + n, OFFS)) for n in (1, 2, 3)]
    for peer in peers:
        pl.semaphore_signal(barrier, inc=1, device_id=peer, device_id_type=MESH)

    def contrib_copy(start, size, sem):
        lanes = pl.ds(pl.multiple_of(start, LANES), size)
        return pltpu.make_async_copy(contrib_ref.at[:, lanes], cbuf.at[:, lanes], sem)

    loads = [
        contrib_copy(core * (E * R - WIDE), WIDE, load_sem.at[0]),
        pltpu.make_async_copy(slot_ref, slots, load_sem.at[1]),
        contrib_copy((1 - core) * WIDE, E * R - WIDE, load_sem.at[2]),
        pltpu.make_async_copy(src_ref, srcv, load_sem.at[3]),
        pltpu.make_async_copy(cls_ref, clsv, load_sem.at[4]),
    ]
    for copy in loads:
        copy.start()

    def trans_copy(g):
        rows = pl.ds(g * GROUP, GROUP)
        return pltpu.make_async_copy(trans_ref.at[rows], traw.at[rows], trans_sem.at[g])

    for g in range(groups):
        trans_copy(g).start()

    cbuf[:, pl.ds(E * R, LANES)] = jnp.zeros((SLOTS, LANES), jnp.float32)
    row = lax.broadcasted_iota(jnp.int32, (8, LANES), 0)
    loads[0].wait()
    loads[1].wait()
    ids = [
        lax.rem(slots[TGT + s] - (dom * TGT - SPILL) + octants, octants)
        for s in range(SLOTS - TGT)
    ]

    def own_half(half, first_point, points_count):
        for n in range(first_point // 8, (first_point + points_count) // 8):
            lanes = pl.ds(pl.multiple_of(half * WIDE, LANES) + n * LANES, LANES)
            points = pl.ds(pl.multiple_of(half * HALF, 8) + n * 8, 8)
            first = pltpu.roll(cbuf[pl.ds(0, 8), lanes], 4, 0)
            second = pltpu.roll(cbuf[pl.ds(8, 8), lanes], 4, 0)
            table = [
                jnp.where(row >= 4, first, 0.0),
                jnp.where(row < 4, first, second),
                jnp.where(row < 4, second, 0.0),
            ]
            for s in range(SLOTS - TGT):
                spill = jnp.broadcast_to(cbuf[pl.ds(TGT + s, 1), lanes], (8, LANES))
                for b in range(3):
                    table[b] = table[b] + jnp.where(row + 8 * b == ids[s], spill, 0.0)
            for b in range(3):
                own[points, pl.ds(b * LANES, LANES)] = block_transpose(table[b])

    def halo_copy(n, k):
        first_point, count = CHUNKS[k]
        rows = pl.ds(pl.multiple_of(core * HALF, HALF) + first_point, count)
        return pltpu.make_async_remote_copy(
            src_ref=own.at[rows, pl.ds((1 - n) * LANES, 2 * LANES)],
            dst_ref=halo.at[n, rows],
            send_sem=halo_send.at[n, k],
            recv_sem=halo_recv.at[n, k],
            device_id=(lax.rem(dom + (1 if n == 0 else parts - 1), parts), across),
            device_id_type=MESH,
        )

    def prepare():
        loads[2].wait()
        own_half(1 - core, 0, HALF)

        loads[3].wait()
        loads[4].wait()
        target = lax.broadcasted_iota(jnp.int32, srcv.shape, 0) + dom * TGT
        code = lax.rem(srcv[...] - target + (REACH + octants), octants) + 1
        spread = (
            lax.broadcasted_iota(jnp.int32, (TGT, TGT * R), 0)
            == lax.broadcasted_iota(jnp.int32, (TGT, TGT * R), 1) // R
        ).astype(jnp.float32)
        dims = (((0,), (0,)), ((), ()))
        code_l = lax.dot_general(
            code.astype(jnp.float32), spread, dims, preferred_element_type=jnp.float32
        )
        class_l = lax.dot_general(
            (clsv[...] - off * classes).astype(jnp.float32), spread, dims,
            preferred_element_type=jnp.float32,
        )

        @pl.loop(0, classes)
        def _(c):
            found = jnp.max(
                jnp.where(class_l == c.astype(jnp.float32), code_l, 0.0), axis=0, keepdims=True
            )
            offs[pl.ds(c, 1), :] = found
            present = jnp.broadcast_to((found > 0.0).astype(jnp.float32), (16, TGT * R))
            for n in range(2):
                masks[c, n] = present[:, n * LANES : (n + 1) * LANES].astype(jnp.bfloat16)

        start = jnp.max(offs[...], axis=1, keepdims=True).astype(jnp.int32) - 1
        codes[...] = jnp.broadcast_to(jnp.clip(start, 0, 2 * REACH), codes.shape)
        code_copy = pltpu.make_async_copy(codes, codes_s, code_sem)
        code_copy.start()

        tpack[...] = jnp.zeros(tpack.shape, jnp.bfloat16)

        @pl.loop(0, groups)
        def _(g):
            trans_copy(g).wait()
            for half in range(2):
                for first_point, count in CHUNKS:
                    begin = half * HALF + first_point
                    size = min(begin + count, E) - begin
                    pieces = []
                    for m in range(GROUP):
                        pieces.append(traw[g * GROUP + m, :, pl.ds(begin, size)])
                        if size < count:
                            pieces.append(jnp.zeros((E, count - size), jnp.float32))
                    lanes = pl.ds(
                        pl.multiple_of(classes * first_point + g * (GROUP * count), LANES),
                        GROUP * count,
                    )
                    for k, term in enumerate(split(jnp.concatenate(pieces, axis=1))):
                        tpack[half, pl.ds(k * EP, E), lanes] = term

        code_copy.wait()

    own_half(core, 0, HALF)
    pl.when(dom == 0)(prepare)
    pl.semaphore_wait(barrier, len(peers))
    sends = [halo_copy(n, 0) for n in range(2)]
    for copy in sends:
        copy.start()
    pl.when(dom != 0)(prepare)

    def forward_copy(n, k):
        first_point, count = CHUNKS[k]
        rows = pl.ds(pl.multiple_of(core * HALF, HALF) + first_point, count)
        return pltpu.make_async_remote_copy(
            src_ref=halo.at[n, rows],
            dst_ref=halo.at[n, rows],
            send_sem=fwd_send.at[n, k],
            recv_sem=fwd_recv.at[n, k],
            device_id=mate,
            device_id_type=MESH,
        )

    forwards = [[forward_copy(n, k) for n in range(2)] for k in range(len(CHUNKS))]

    lane16 = lax.broadcasted_iota(jnp.int32, (16, LANES), 1)
    lhalo, rhalo = halo.at[0], halo.at[1]

    def shifted(half, k, left):
        first_point, count = CHUNKS[k]
        for b in range(first_point // 16, (first_point + count) // 16):
            rows = pl.ds(pl.multiple_of(half * HALF, 16) + b * 16, 16)

            def tile(ref, q):
                return ref[rows, pl.ds(q * LANES, LANES)]

            if left:
                first_tile = 0
                window = [tile(lhalo, 0), tile(lhalo, 1) + tile(own, 0), tile(own, 1)]
            else:
                first_tile = 2
                window = [tile(own, 1), tile(own, 2) + tile(rhalo, 0), tile(rhalo, 1)]
            for term, terms in enumerate(zip(*map(split, window))):
                for s in range(8):
                    shift = LANES - R * s
                    if s == 0:
                        tiles = terms[:2] if left else terms
                    else:
                        rolled = [pltpu.roll(w, shift, 1) for w in terms]
                        tiles = [
                            jnp.where(lane16 < shift, rolled[q], rolled[q + 1]) for q in range(2)
                        ]
                    for q, value in enumerate(tiles):
                        ywin[s * 5 + first_tile + q, rows, pl.ds(term * LANES, LANES)] = value

    def stacked(half, k, n, chosen):
        first_point, count = CHUNKS[k]
        rows = pl.ds(pl.multiple_of(half * HALF, 16) + first_point, count)
        values = []
        for c in chosen:
            begin = codes_s[c, 0]
            at = lax.rem(begin, 8) * 5 + begin // 8
            mask = masks[c, n]
            both = jnp.concatenate([mask, mask], axis=1)
            value = ywin[at + n, rows, :].reshape(count // 16, 16, 2 * LANES) * both[None]
            values.append(value.reshape(count, 2 * LANES))
        return jnp.concatenate(values, axis=0)

    def product(half, k, n, total):
        first_point, count = CHUNKS[k]
        for c in range(0, classes, 2 * GROUP):
            chosen = range(c, min(c + 2 * GROUP, classes))
            lanes = pl.ds(classes * first_point + c * count, len(chosen) * count)
            prod = jnp.dot(
                tpack[half, :, lanes], stacked(half, k, n, chosen),
                preferred_element_type=jnp.float32,
            )
            total = total + (prod[:EP, :LANES] + (prod[EP:, :LANES] + prod[:EP, LANES:]))
        return total

    lane8 = lax.broadcasted_iota(jnp.int32, (8, LANES), 1)

    def to_send(n, value):
        for g in range(TILES // 2):
            a, b = (value[(2 * g + k) * 8 : (2 * g + k + 1) * 8] for k in range(2))
            rows = pl.ds(g * 8, 8)
            sendbuf[2 * n, rows, :] = jnp.where(lane8 < 64, a, pltpu.roll(b, 64, 1))
            sendbuf[2 * n + 1, rows, :] = jnp.where(lane8 < 64, pltpu.roll(a, 64, 1), b)

    def final_copy(peer):
        n = lax.rem(peer - off + OFFS, OFFS)
        return pltpu.make_async_remote_copy(
            src_ref=sendbuf.at[peer],
            dst_ref=recvbuf.at[n],
            send_sem=rs_send.at[n - 1],
            recv_sem=rs_recv.at[n - 1],
            device_id=(dom, peer),
            device_id_type=MESH,
        )

    chip = off // 2
    total = jnp.zeros((EP, LANES), jnp.float32)
    for n in (1, 0):
        sends[n].wait_recv()
        forwards[0][n].start()
        shifted(core, 0, n == 0)
        if n == 0:
            total = product(core, 0, 1 - chip, total)
        forwards[0][n].wait_recv()
        shifted(1 - core, 0, n == 0)
    total = product(1 - core, 0, 1 - chip, total)
    to_send(1 - chip, total)
    finals = [final_copy(2 * (1 - chip) + k) for k in (1, 0)]
    for copy in finals:
        copy.start()
    total = jnp.zeros((EP, LANES), jnp.float32)
    for half in range(2):
        for k in range(len(CHUNKS)):
            total = product(half, k, chip, total)
    to_send(chip, total)
    finals.append(final_copy(2 * chip + 1 - core))
    finals[2].start()
    for n in (1, 2, 3):
        final_copy(lax.rem(off + n, OFFS)).wait_recv()
    for g in range(TILES // 2):
        rows = pl.ds(g * 8, 8)
        value = block_transpose(
            (sendbuf[off, rows, :] + recvbuf[1, rows, :]) + (recvbuf[2, rows, :] + recvbuf[3, rows, :])
        )
        for n in range(2):
            if 2 * g + n < E // 8:
                part = value[n * TGT // OFFS : (n + 1) * TGT // OFFS]
                out_ref[:, pl.ds((2 * g + n) * LANES, LANES)] = part
    for copy in sends + forwards[0] + finals:
        copy.wait_send()


def solution(mesh):
    parts = mesh.shape["dom"]

    def local(contrib, slot_octant, vlist_src, vlist_class, translation):
        classes = translation.shape[0]
        wide = TGT * R
        hbm_spec = pl.BlockSpec(memory_space=pltpu.HBM)

        args = (contrib, slot_octant, vlist_src, vlist_class, translation)
        args = [pltpu.with_memory_space_constraint(a, pltpu.HBM) for a in args]

        def body(*refs):
            kernel(parts, *refs)

        vmem_spec = pl.BlockSpec(memory_space=pltpu.VMEM)
        total = pl.pallas_call(
            body,
            out_shape=jax.ShapeDtypeStruct((TGT // OFFS, E * R), jnp.float32),
            in_specs=[hbm_spec] * 5,
            out_specs=vmem_spec,
            scratch_shapes=[
                pltpu.VMEM((SLOTS, TILES * LANES), jnp.float32),
                pltpu.SMEM((SLOTS,), jnp.int32),
                pltpu.VMEM(vlist_src.shape, jnp.int32),
                pltpu.VMEM(vlist_class.shape, jnp.int32),
                pltpu.VMEM(translation.shape, jnp.float32),
                pltpu.VMEM((2, 2 * EP, classes * HALF), jnp.bfloat16),
                pltpu.VMEM((EP, 3 * LANES), jnp.float32),
                pltpu.VMEM((2, EP, 2 * LANES), jnp.float32),
                pltpu.VMEM((40, EP, 2 * LANES), jnp.bfloat16),
                pltpu.VMEM((classes, wide), jnp.float32),
                pltpu.VMEM((classes, 2, 16, LANES), jnp.bfloat16),
                pltpu.VMEM((classes, LANES), jnp.int32),
                pltpu.SMEM((classes, LANES), jnp.int32),
                pltpu.VMEM((OFFS, HALF, LANES), jnp.float32),
                pltpu.VMEM((OFFS, HALF, LANES), jnp.float32),
                pltpu.SemaphoreType.DMA((5,)),
                pltpu.SemaphoreType.DMA((classes // GROUP,)),
                pltpu.SemaphoreType.DMA((2, 2)),
                pltpu.SemaphoreType.DMA((2, 2)),
                pltpu.SemaphoreType.DMA((2, 2)),
                pltpu.SemaphoreType.DMA((2, 2)),
                pltpu.SemaphoreType.DMA(()),
                pltpu.SemaphoreType.DMA((3,)),
                pltpu.SemaphoreType.DMA((3,)),
            ],
            compiler_params=pltpu.CompilerParams(
                collective_id=0, has_side_effects=True, vmem_limit_bytes=32 << 20
            ),
        )(*args)
        return total

    return jax.shard_map(
        local,
        mesh=mesh,
        in_specs=(P("dom", None), P("dom"), P("dom", None), P("dom", None), P("off", None, None)),
        out_specs=P(("dom", "off"), None),
        check_vma=False,
    )
```
